128 devices in a mesh: row: 16 (over z, y), col: 8 (over x, core).
Axes of the slice: x: 4, y: 4, z: 4, core: 2. Of those that a mesh axis runs over, the one named last changes fastest.
Arguments:
- struct_disp: float32 [48, 32768], P(None, ('row', 'col')), may hold values from -6 to 6
- target: int32 [32768], P(('row', 'col')), may hold values from 0 to 32767, as said below
- inverse: bfloat16 [32768, 32768], P('row', 'col'), may hold values from -0.046875 to 0.046875
- centre_xyz: float32 [3, 32768], replicated, may hold values from 0 to 1, as said below
- node_xyz: float32 [3, 262144], P(None, ('row', 'col')), may hold values from 0 to 1, as said below
Outputs:
- volume_disp: float32 [48, 262144], P(None, ('row', 'col'))
The draws below stay inside these ranges and needn't reach their ends.
Inputs may be any that keep to these rules, and one draw needn't show every extreme that they name: `target`: centre j is held by the owner of index r * 8 + c with c = j // 4096 and r = (j % 4096) // 256. The 256 entries of one device name centres of at most 4 entries for any one owner, and one owner receives exactly 4 entries from every device. `centre_xyz`: every centre lies on the boundary of the cube that spans 0.3 to 0.7 in each coordinate. `node_xyz`: every volume node lies outside the cube that spans 0.3 to 0.7 in each coordinate, or on its boundary.
All inputs are finite; a program needn't handle non-finite values.
Results may differ from the reference program's by a relative error of at most 0.0049.
Values may be sent and summed in bfloat16 or wider, within the bound.
No kernel may reach another device: no remote copies, remote signals or barrier semaphores. Data moves between devices by JAX's collectives and lax.ppermute only.
A program may use at most 64 MiB of HBM per device.

```python
import math
import jax
import jax.numpy as jnp
from jax import lax

M = 32768
E_DEV = 256
DISP_ROWS = 48
OWNERS = 128
CAP = 4
ENTRIES = 32768
VOL = 262144
BLK = 256
CB = 4096
N_COL = 8


def draw_target(key, part):
    first_key, second_key, third_key = jax.random.split(jax.random.fold_in(key, 11), 3)
    hot_owner = jax.random.randint(first_key, (), 0, OWNERS)
    sender_keys = jax.random.split(second_key, OWNERS)
    orders = jax.vmap(lambda sender_key: jax.random.permutation(sender_key, OWNERS - 1))(sender_keys)
    others = orders + (orders >= hot_owner).astype(jnp.int32)
    positions = jnp.arange(E_DEV, dtype=jnp.int32)
    rest_pos = jnp.maximum(positions - CAP, 0) % (OWNERS - 1)
    rest_dest = jnp.take_along_axis(others, jnp.broadcast_to(rest_pos[None, :], (OWNERS, E_DEV)), axis=1)
    destination = jnp.where(positions[None, :] < CAP, hot_owner, rest_dest)
    owner_row = destination // N_COL
    owner_col = destination % N_COL
    within = jax.random.randint(third_key, (OWNERS, E_DEV), 0, BLK)
    return (owner_col * CB + owner_row * BLK + within).reshape(-1).astype(jnp.int32)


def face_points(key, how_many, lift_scale):
    face_key, one_key, two_key, lift_key = jax.random.split(key, 4)
    face_ids = jax.random.randint(face_key, (how_many,), 0, 6)
    normal_ids = face_ids // 2
    side_ids = face_ids % 2
    along_one = 0.3 + 0.4 * jax.random.uniform(one_key, (how_many,), jnp.float32)
    along_two = 0.3 + 0.4 * jax.random.uniform(two_key, (how_many,), jnp.float32)
    lift_off = lift_scale * jax.random.uniform(lift_key, (how_many,), jnp.float32)
    plane_at = jnp.where(side_ids == 1, 0.7 + lift_off, 0.3 - lift_off)
    coord_x = jnp.where(normal_ids == 0, plane_at, along_one)
    coord_y = jnp.where(normal_ids == 0, along_one, jnp.where(normal_ids == 1, plane_at, along_two))
    coord_z = jnp.where(normal_ids == 2, plane_at, along_two)
    return jnp.stack([coord_x, coord_y, coord_z], axis=0).astype(jnp.float32)


def draw_centre_xyz(key, part):
    return face_points(jax.random.fold_in(key, 21), M, 0.0)


def draw_node_xyz(key, part):
    support = 2.0 / math.sqrt(M)
    lift_scale = 0.6 * support
    return face_points(jax.random.fold_in(key, 37), VOL, lift_scale)


def with_spikes(entries, own_key, source, target, blocks, factor):
    owner, partner = [(jnp.arange(entries.shape[position]) // (entries.shape[position] // blocks)).reshape([-1 if axis == position else 1 for axis in range(entries.ndim)]) for position in (source, target)]
    chosen = jax.random.permutation(own_key, blocks)[partner]
    strong = (owner == chosen) | (owner == (partner + blocks // 2) % blocks)
    return jnp.where(strong, factor * entries, entries)


def steps_of(rng, dims, shards, smallest, largest):
    def one(axis_at, parts):
        heights = jax.random.uniform(jax.random.fold_in(jax.random.fold_in(rng, 6), axis_at), (parts,), jnp.float32, smallest / len(shards), largest / len(shards))
        return jnp.repeat(jnp.exp(heights), dims[axis_at] // parts).reshape((-1,) + (1,) * (len(dims) - axis_at - 1))

    gain = one(*shards[0])
    for cut in shards[1:]:
        gain = gain * one(*cut)
    return gain


def gaussian(rng, extent, spread, most, pieces=(), held_as=jnp.bfloat16):
    values = jax.random.normal(rng, extent, jnp.float32) * spread
    if len(pieces) > 0:
        values = steps_of(rng, extent, pieces, -0.22, 0.18) * values
    return jnp.clip(values, min=-most, max=most).astype(held_as)


def gaussian_with(key, extent, scale, limit, shards, heavy, kind=jnp.bfloat16):
    values = scale * jax.random.normal(key, extent, jnp.float32)
    if shards:
        values = values * steps_of(key, extent, shards, -0.22, 0.18)
    return jnp.clip(with_spikes(values, jax.random.fold_in(key, 3), *heavy), -limit, limit).astype(kind)


def setup_inputs(seed: int = 0) -> dict:
    arg_keys = jax.random.split(jax.random.key(seed), 6)
    return {
        "struct_disp": gaussian(arg_keys[0], (DISP_ROWS, ENTRIES), 1.0, 6.0, ((1, 128),), jnp.float32),
        "target": draw_target(jax.random.fold_in(arg_keys[5], 71), 0),
        "inverse": gaussian_with(arg_keys[2], (M, M), ENTRIES ** -0.5, 0.046875, ((0, 16), (1, 8)), (1, 0, 16, 2.0)),
        "centre_xyz": draw_centre_xyz(jax.random.fold_in(arg_keys[5], 71), 0),
        "node_xyz": draw_node_xyz(jax.random.fold_in(arg_keys[5], 71), 0),
    }


def wendland_tile(centre_block, node_block):
    radius = 2.0 / math.sqrt(M)
    squared = jnp.zeros((centre_block.shape[1], node_block.shape[1]), jnp.float32)
    for component in range(3):
        difference = centre_block[component][:, None] - node_block[component][None, :]
        squared = squared + difference * difference
    scaled = jnp.sqrt(squared) / radius
    remain = jnp.maximum(1.0 - scaled, 0.0)
    return (remain ** 4 * (4.0 * scaled + 1.0)).astype(jnp.bfloat16)

def reference(struct_disp, target, inverse, centre_xyz, node_xyz):
    centre_disp = jnp.zeros((DISP_ROWS, M), jnp.float32).at[:, target].add(struct_disp)
    disp_bf = centre_disp.astype(jnp.bfloat16)
    coefs = lax.dot_general(disp_bf, inverse, (((1,), (1,)), ((), ())), preferred_element_type=jnp.float32)
    coef_bf = coefs.astype(jnp.bfloat16)
    block_size = math.gcd(VOL, 1024)
    node_blocks = node_xyz.reshape(3, VOL // block_size, block_size).transpose(1, 0, 2)

    def one_block(nodes):
        kernel_tile = wendland_tile(centre_xyz, nodes)
        return jnp.dot(coef_bf, kernel_tile, preferred_element_type=jnp.float32)
    blocks_out = lax.map(one_block, node_blocks)
    return blocks_out.transpose(1, 0, 2).reshape(DISP_ROWS, VOL)
```

```python
import math

import jax
import jax.numpy as jnp
from jax import lax
from jax.sharding import PartitionSpec as P

M = 32768
CAP = 4


def wendland_tile(centre_block, node_block):
    radius = 2.0 / math.sqrt(M)
    squared = jnp.zeros((centre_block.shape[1], node_block.shape[1]), jnp.float32)
    for component in range(3):
        difference = centre_block[component][:, None] - node_block[component][None, :]
        squared = squared + difference * difference
    scaled = jnp.sqrt(squared) / radius
    remain = jnp.maximum(1.0 - scaled, 0.0)
    return (remain**4 * (4.0 * scaled + 1.0)).astype(jnp.bfloat16)


def exchange(value, axes):
    return lax.all_to_all(value, axes, split_axis=0, concat_axis=0, tiled=True)


def column_displacements(struct_disp, target, rows, cols, col_block):
    disp_rows, entries = struct_disp.shape
    owner_block = col_block // rows
    owner_col = target // col_block
    owner_row = target % col_block // owner_block
    offsets = target % owner_block
    owner = owner_row * cols + owner_col
    position = jnp.arange(entries, dtype=jnp.int32)
    earlier = (owner[:, None] == owner[None, :]) & (position[:, None] < position[None, :])
    rank = jnp.sum(earlier.astype(jnp.int32), axis=0)
    slots = rows * CAP
    slot = owner_col * slots + owner_row * CAP + rank
    pick = (jnp.arange(cols * slots, dtype=jnp.int32)[:, None] == slot[None, :]).astype(jnp.bfloat16)
    payload = jnp.concatenate(
        [
            struct_disp.astype(jnp.bfloat16),
            offsets.astype(jnp.bfloat16)[None, :],
            jnp.zeros((64 - disp_rows - 1, entries), jnp.bfloat16),
        ],
        axis=0,
    )
    packed = lax.dot_general(
        pick, payload, (((1,), (1,)), ((), ())), preferred_element_type=jnp.float32
    ).astype(jnp.bfloat16)
    packed = packed.reshape(cols, slots, 64)
    half = slots // 2
    packed = jnp.concatenate([packed[:, :half], packed[:, half:]], axis=-1)
    send = jnp.broadcast_to(packed[None], (rows, cols, half, 128)).reshape(rows * cols, half, 128)
    recv = exchange(send, ("row", "col"))
    recv = recv.reshape(rows * cols, rows // 2, CAP, 128).transpose(1, 0, 2, 3)
    recv = recv.reshape(rows // 2, rows * cols * CAP, 128)
    columns = jnp.arange(owner_block, dtype=jnp.int32).astype(jnp.bfloat16)
    halves = []
    for side in range(2):
        part = recv[:, :, side * 64 : side * 64 + 64]
        place = (part[:, :, disp_rows : disp_rows + 1] == columns[None, None, :]).astype(jnp.bfloat16)
        halves.append(
            lax.dot_general(
                part[:, :, :disp_rows],
                place,
                (((1,), (1,)), ((0,), (0,))),
                preferred_element_type=jnp.float32,
            )
        )
    summed = jnp.concatenate(halves, axis=0).astype(jnp.bfloat16)
    return summed.transpose(1, 0, 2).reshape(disp_rows, col_block)


def per_device(struct_disp, target, inverse, centre_xyz, node_xyz):
    rows = lax.axis_size("row")
    cols = lax.axis_size("col")
    row_block, col_block = inverse.shape
    disp_rows = struct_disp.shape[0]
    nodes = node_xyz.shape[1]
    piece = row_block // cols
    col_index = lax.axis_index("col")

    peer_nodes = lax.all_gather(node_xyz, "col", axis=0)
    disp_bf = column_displacements(struct_disp, target, rows, cols, col_block)
    partial = lax.dot_general(
        disp_bf, inverse, (((1,), (1,)), ((), ())), preferred_element_type=jnp.float32
    )
    partial = partial.astype(jnp.bfloat16).reshape(disp_rows, cols, piece).transpose(1, 0, 2)
    coef = jnp.sum(exchange(partial, "col").astype(jnp.float32), axis=0).astype(jnp.bfloat16)
    coefs = exchange(jnp.broadcast_to(coef[None], (rows,) + coef.shape), "row")
    coefs = coefs.transpose(1, 0, 2).reshape(disp_rows, rows * piece)
    centres = lax.dynamic_index_in_dim(
        centre_xyz.reshape(3, rows, cols, piece), col_index, 2, keepdims=False
    ).reshape(3, rows * piece)

    def one_peer(counter, outs):
        tile = wendland_tile(centres, peer_nodes[counter])
        part = jnp.dot(coefs, tile, preferred_element_type=jnp.float32)
        return lax.dynamic_update_index_in_dim(outs, part.astype(jnp.bfloat16), counter, 0)

    outs = lax.fori_loop(0, cols, one_peer, jnp.zeros((cols, disp_rows, nodes), jnp.bfloat16))
    return jnp.sum(exchange(outs, "col").astype(jnp.float32), axis=0)


def solution(mesh):
    placed = (
        P(None, ("row", "col")),
        P(("row", "col")),
        P("row", "col"),
        P(),
        P(None, ("row", "col")),
    )
    return jax.shard_map(
        per_device, mesh=mesh, in_specs=placed, out_specs=P(None, ("row", "col")), check_vma=False
    )
```

```python
import math

import jax
import jax.numpy as jnp
from jax import lax
from jax.experimental import pallas as pl
from jax.experimental.pallas import tpu as pltpu
from jax.sharding import PartitionSpec as P

M = 32768
CAP = 4
RADIUS = 2.0 / math.sqrt(M)
SCALE = 4.0 / RADIUS
GROUP = 16
BATCH = 16
LANES = 128
FAR = 1.0e6


def exchange(value, axes):
    return lax.all_to_all(value, axes, split_axis=0, concat_axis=0, tiled=True)


def column_displacements(struct_disp, target, rows, cols, col_block):
    disp_rows, entries = struct_disp.shape
    owner_block = col_block // rows
    owner_col = target // col_block
    owner_row = target % col_block // owner_block
    offsets = target % owner_block
    owner = owner_row * cols + owner_col
    position = jnp.arange(entries, dtype=jnp.int32)
    earlier = (owner[:, None] == owner[None, :]) & (position[:, None] < position[None, :])
    rank = jnp.sum(earlier.astype(jnp.int32), axis=0)
    slots = rows * CAP
    slot = owner_col * slots + owner_row * CAP + rank
    pick = (jnp.arange(cols * slots, dtype=jnp.int32)[:, None] == slot[None, :]).astype(jnp.bfloat16)
    payload = jnp.concatenate(
        [
            struct_disp.astype(jnp.bfloat16),
            offsets.astype(jnp.bfloat16)[None, :],
            jnp.zeros((64 - disp_rows - 1, entries), jnp.bfloat16),
        ],
        axis=0,
    )
    packed = lax.dot_general(
        pick, payload, (((1,), (1,)), ((), ())), preferred_element_type=jnp.float32
    ).astype(jnp.bfloat16)
    packed = packed.reshape(cols, slots, 64)
    half = slots // 2
    packed = jnp.concatenate([packed[:, :half], packed[:, half:]], axis=-1)
    send = jnp.broadcast_to(packed[None], (rows, cols, half, 128)).reshape(rows * cols, half, 128)
    recv = exchange(send, ("row", "col"))
    recv = recv.reshape(rows * cols, rows // 2, CAP, 128).transpose(1, 0, 2, 3)
    recv = recv.reshape(rows // 2, rows * cols * CAP, 128)
    columns = jnp.arange(owner_block, dtype=jnp.int32).astype(jnp.bfloat16)
    halves = []
    for side in range(2):
        part = recv[:, :, side * 64 : side * 64 + 64]
        place = (part[:, :, disp_rows : disp_rows + 1] == columns[None, None, :]).astype(jnp.bfloat16)
        halves.append(
            lax.dot_general(
                part[:, :, :disp_rows],
                place,
                (((1,), (1,)), ((0,), (0,))),
                preferred_element_type=jnp.float32,
            )
        )
    summed = jnp.concatenate(halves, axis=0).astype(jnp.bfloat16)
    return summed.transpose(1, 0, 2).reshape(disp_rows, col_block)


def surface_key(xyz):
    bits = 6
    side = 1 << bits
    offset = xyz - 0.5
    size = jnp.abs(offset)
    on_x = (size[0] >= size[1]) & (size[0] >= size[2])
    on_y = jnp.logical_not(on_x) & (size[1] >= size[2])
    normal = jnp.where(on_x, offset[0], jnp.where(on_y, offset[1], offset[2]))
    face = jnp.where(on_x, 0, jnp.where(on_y, 2, 4)) + (normal > 0).astype(jnp.int32)
    along = [jnp.where(on_x, xyz[1], xyz[0]), jnp.where(on_x | on_y, xyz[2], xyz[1])]
    u, v = [jnp.clip((side * (w - 0.3) / 0.4).astype(jnp.int32), 0, side - 1) for w in along]
    code = jnp.zeros_like(u)
    for bit in reversed(range(bits)):
        step = 1 << bit
        u_on = (u >> bit) & 1
        v_on = (v >> bit) & 1
        code = code + step * step * ((3 * u_on) ^ v_on)
        flip = (v_on == 0) & (u_on == 1)
        u, v = jnp.where(flip, side - 1 - u, u), jnp.where(flip, side - 1 - v, v)
        u, v = jnp.where(v_on == 0, v, u), jnp.where(v_on == 0, u, v)
    return face * side * side + code


def sorted_rank(xyz):
    count = xyz.shape[1]
    key = surface_key(xyz) * count + jnp.arange(count, dtype=jnp.int32)
    return jnp.sum((key[:, None] < key[None, :]).astype(jnp.int32), axis=0)


def pick_columns(xyz, pick):
    high = lax.reduce_precision(xyz, 8, 7)
    middle = lax.reduce_precision(xyz - high, 8, 7)
    low = xyz - high - middle
    parts = jnp.concatenate([high, middle, low], axis=0).astype(jnp.bfloat16)
    picked = jnp.dot(parts, pick, preferred_element_type=jnp.float32)
    return picked[0:3] + picked[3:6] + picked[6:9]


def with_boxes(xyz, size):
    count = xyz.shape[1]
    runs = xyz.reshape(3, count // size, size)
    boxes = jnp.concatenate([jnp.min(runs, axis=2), jnp.max(runs, axis=2)], axis=0).reshape(-1)
    row = jnp.pad(boxes, (0, count - boxes.shape[0]))
    return jnp.concatenate([xyz, row[None, :]], axis=0)


def near_groups(centre_data, node_data):
    rows, _, piece = centre_data.shape
    cols, _, nodes = node_data.shape
    halves = piece // LANES
    groups = nodes // GROUP
    centre_box = centre_data[:, 3, : 6 * halves].reshape(rows, 6, halves)
    node_box = node_data[:, 3, : 6 * groups].reshape(cols, 6, groups).transpose(1, 0, 2).reshape(6, -1)
    total = cols * groups
    apart = jnp.zeros((rows, halves, total), jnp.float32)
    for axis in range(3):
        low = centre_box[:, axis, :, None] - node_box[None, None, 3 + axis, :]
        high = node_box[None, None, axis, :] - centre_box[:, 3 + axis, :, None]
        gap = jnp.maximum(jnp.maximum(low, high), 0.0)
        apart = apart + gap * gap
    near = jnp.any(apart <= RADIUS * RADIUS * 1.001, axis=0)
    upto = (jnp.arange(total)[:, None] <= jnp.arange(total)[None, :]).astype(jnp.bfloat16)
    place = jnp.dot(near.astype(jnp.bfloat16), upto, preferred_element_type=jnp.float32)
    counts = place[:, -1].astype(jnp.int32)
    place = jnp.where(near, place.astype(jnp.int32) - 1, -1)
    slots = jnp.arange(total + BATCH, dtype=jnp.int32)
    hit = place[:, :, None] == slots[None, None, :]
    number = jnp.arange(total, dtype=jnp.int32)
    listed = jnp.sum(jnp.where(hit, number[None, :, None], 0), axis=1)
    return counts, jnp.where(slots[None, :] < counts[:, None], listed, total)


def interpolate(counts, lists, node_rows, centre_data, coefs, cols):
    rows, disp_rows, piece = coefs.shape
    total = node_rows.shape[0] - GROUP
    nodes = total // cols
    halves = piece // LANES

    def kernel(count_ref, list_ref, node_ref, centre_ref, coef_ref, out_ref, acc_ref):
        def clear(step, carry):
            acc_ref[pl.ds(pl.multiple_of(step * 128, 128), 128), :] = jnp.zeros((128, LANES), jnp.float32)
            return carry

        lax.fori_loop(0, total // 128, clear, 0)
        acc_ref[total:, :] = jnp.zeros((GROUP, LANES), jnp.float32)

        for half in range(halves):
            lanes = slice(half * LANES, (half + 1) * LANES)

            def batch(step, carry):
                starts = [
                    pl.multiple_of(list_ref[half, step * BATCH + i] * GROUP, GROUP) for i in range(BATCH)
                ]
                node = jnp.concatenate([node_ref[pl.ds(start, GROUP), :] for start in starts], axis=0)
                node = [jnp.broadcast_to(node[:, a : a + 1], (GROUP * BATCH, LANES)) for a in range(3)]
                total_part = jnp.zeros((GROUP * BATCH, disp_rows), jnp.float32)
                for pair in range(rows // 2):
                    tiles = []
                    for run in (2 * pair, 2 * pair + 1):
                        squared = None
                        for axis in range(3):
                            difference = node[axis] - centre_ref[run, axis : axis + 1, lanes]
                            square = difference * difference
                            squared = square if squared is None else squared + square
                        scaled = squared * lax.rsqrt(jnp.maximum(squared, 1e-30))
                        remain = jnp.maximum(4.0 - scaled, 0.0)
                        remain = remain * remain
                        tiles.append((remain * remain * (scaled + 1.0)).astype(jnp.bfloat16))
                    weights = jnp.concatenate(
                        [coef_ref[2 * pair, :, lanes], coef_ref[2 * pair + 1, :, lanes]], axis=1
                    )
                    total_part = total_part + lax.dot_general(
                        jnp.concatenate(tiles, axis=1),
                        weights,
                        (((1,), (1,)), ((), ())),
                        preferred_element_type=jnp.float32,
                    )
                for i, start in enumerate(starts):
                    acc_ref[pl.ds(start, GROUP), :disp_rows] += total_part[i * GROUP : (i + 1) * GROUP]
                return carry

            lax.fori_loop(0, (count_ref[half] + BATCH - 1) // BATCH, batch, 0)

        lane = lax.broadcasted_iota(jnp.int32, (128, LANES), 1)
        for col in range(cols):

            def pack(step, carry):
                first = pl.multiple_of(step * 128, 128)
                low = acc_ref[pl.ds(col * nodes + first, 128), :]
                high = acc_ref[pl.ds(col * nodes + nodes // 2 + first, 128), :]
                both = jnp.where(lane < LANES // 2, low, pltpu.roll(high, LANES // 2, 1))
                out_ref[col, pl.ds(first, 128), :] = both.astype(jnp.bfloat16)
                return carry

            lax.fori_loop(0, nodes // 256, pack, 0)

    vmem = pl.BlockSpec(memory_space=pltpu.VMEM)
    smem = pl.BlockSpec(memory_space=pltpu.SMEM)
    return pl.pallas_call(
        kernel,
        out_shape=jax.ShapeDtypeStruct((cols, nodes // 2, LANES), jnp.bfloat16),
        in_specs=[smem, smem, vmem, vmem, vmem],
        out_specs=vmem,
        scratch_shapes=[pltpu.VMEM((total + GROUP, LANES), jnp.float32)],
        name="interpolate",
    )(counts, lists, node_rows, centre_data, coefs)


def per_device(struct_disp, target, inverse, centre_xyz, node_xyz):
    rows = lax.axis_size("row")
    cols = lax.axis_size("col")
    row_block, col_block = inverse.shape
    disp_rows = struct_disp.shape[0]
    nodes = node_xyz.shape[1]
    piece = row_block // cols

    disp_bf = column_displacements(struct_disp, target, rows, cols, col_block)

    own_xyz = lax.dynamic_slice_in_dim(centre_xyz, lax.axis_index("row") * row_block, row_block, 1)
    centre_rank = sorted_rank(own_xyz)
    order = jnp.arange(row_block, dtype=jnp.int32)
    centre_pick = (centre_rank[:, None] == order[None, :]).astype(jnp.bfloat16)
    piece_order = lax.axis_index("col") * piece + jnp.arange(piece, dtype=jnp.int32)
    piece_pick = (centre_rank[:, None] == piece_order[None, :]).astype(jnp.bfloat16)
    piece_data = with_boxes(pick_columns(own_xyz, piece_pick), LANES)
    centre_data = exchange(jnp.broadcast_to(piece_data[None], (rows, 4, piece)), "row")

    node_rank = sorted_rank(node_xyz)
    node_order = jnp.arange(nodes, dtype=jnp.int32)
    node_pick = (node_rank[:, None] == node_order[None, :]).astype(jnp.bfloat16)
    own_nodes = with_boxes(pick_columns(node_xyz, node_pick), GROUP)
    node_data = exchange(jnp.broadcast_to(own_nodes[None], (cols, 4, nodes)), "col")

    counts, lists = near_groups(centre_data, node_data)
    node_rows = node_data[:, :3].transpose(0, 2, 1).reshape(cols * nodes, 3) * SCALE
    node_rows = jnp.pad(node_rows, ((0, GROUP), (0, 0)), constant_values=FAR)

    partial = lax.dot_general(
        disp_bf, inverse, (((1,), (1,)), ((), ())), preferred_element_type=jnp.float32
    )
    partial = jnp.dot(partial.astype(jnp.bfloat16), centre_pick, preferred_element_type=jnp.float32)
    partial = partial.astype(jnp.bfloat16).reshape(disp_rows, cols, piece).transpose(1, 0, 2)
    coef = jnp.sum(exchange(partial, "col").astype(jnp.float32), axis=0).astype(jnp.bfloat16)
    coefs = exchange(jnp.broadcast_to(coef[None], (rows,) + coef.shape), "row")

    outs = interpolate(counts, lists, node_rows, centre_data[:, :3] * SCALE, coefs, cols)
    summed = jnp.sum(exchange(outs, "col").astype(jnp.float32), axis=0)
    ordered = jnp.concatenate([summed[:, :disp_rows], summed[:, 64 : 64 + disp_rows]], axis=0)
    ordered = (ordered * (1.0 / 256.0)).astype(jnp.bfloat16)
    return lax.dot_general(
        ordered, node_pick, (((0,), (1,)), ((), ())), preferred_element_type=jnp.float32
    )


def solution(mesh):
    placed = (
        P(None, ("row", "col")),
        P(("row", "col")),
        P("row", "col"),
        P(),
        P(None, ("row", "col")),
    )
    return jax.shard_map(
        per_device, mesh=mesh, in_specs=placed, out_specs=P(None, ("row", "col")), check_vma=False
    )
```

```python
import math

import jax
import jax.numpy as jnp
from jax import lax
from jax.experimental import pallas as pl
from jax.experimental.pallas import tpu as pltpu
from jax.sharding import PartitionSpec as P

M = 32768
CAP = 4
RADIUS = 2.0 / math.sqrt(M)
SCALE = 4.0 / RADIUS
GROUP = 8
BATCH = 32
LANES = 128
BLOCK = 32
BOX = 16
FACES = (
    (1, 0, (0, 0, 0), 0),
    (2, 0, (1, 0, 0), 0),
    (0, 0, (0, 0, 0), 1),
    (1, 1, (0, 1, 0), 0),
    (0, 1, (1, 1, 0), 2),
    (2, 1, (1, 1, 1), 0),
)


def exchange(value, axes):
    return lax.all_to_all(value, axes, split_axis=0, concat_axis=0, tiled=True)


def routed_entries(struct_disp, target, rows, cols, col_block):
    disp_rows, entries = struct_disp.shape
    owner_block = col_block // rows
    owner_col = target // col_block
    owner_row = target % col_block // owner_block
    offsets = target % owner_block
    owner = owner_row * cols + owner_col
    position = jnp.arange(entries, dtype=jnp.int32)
    earlier = (owner[:, None] == owner[None, :]) & (position[:, None] < position[None, :])
    rank = jnp.sum(earlier.astype(jnp.int32), axis=0)
    slots = rows * CAP
    slot = owner_col * slots + owner_row * CAP + rank
    pick = (jnp.arange(cols * slots, dtype=jnp.int32)[:, None] == slot[None, :]).astype(jnp.bfloat16)
    payload = jnp.concatenate(
        [
            struct_disp.astype(jnp.bfloat16),
            offsets.astype(jnp.bfloat16)[None, :],
            jnp.zeros((64 - disp_rows - 1, entries), jnp.bfloat16),
        ],
        axis=0,
    )
    packed = lax.dot_general(
        pick, payload, (((1,), (1,)), ((), ())), preferred_element_type=jnp.float32
    ).astype(jnp.bfloat16)
    packed = packed.reshape(cols, slots, 64)
    half = slots // 2
    packed = jnp.concatenate([packed[:, :half], packed[:, half:]], axis=-1)
    return jnp.broadcast_to(packed[None], (rows, cols, half, 128)).reshape(rows * cols, half, 128)


def column_displacements(recv, disp_rows, rows, cols, col_block):
    owner_block = col_block // rows
    recv = recv.reshape(rows * cols, rows // 2, CAP, 128).transpose(1, 0, 2, 3)
    recv = recv.reshape(rows // 2, rows * cols * CAP, 128)
    columns = jnp.arange(owner_block, dtype=jnp.int32).astype(jnp.bfloat16)
    halves = []
    for side in range(2):
        part = recv[:, :, side * 64 : side * 64 + 64]
        place = (part[:, :, disp_rows : disp_rows + 1] == columns[None, None, :]).astype(jnp.bfloat16)
        halves.append(
            lax.dot_general(
                part[:, :, :disp_rows],
                place,
                (((1,), (1,)), ((0,), (0,))),
                preferred_element_type=jnp.float32,
            )
        )
    summed = jnp.concatenate(halves, axis=0).astype(jnp.bfloat16)
    return summed.transpose(1, 0, 2).reshape(disp_rows, col_block)


def surface_key(xyz):
    bits = 6
    side = 1 << bits
    offset = xyz - 0.5
    size = jnp.abs(offset)
    on_x = (size[0] >= size[1]) & (size[0] >= size[2])
    on_y = jnp.logical_not(on_x) & (size[1] >= size[2])
    normal = jnp.where(on_x, offset[0], jnp.where(on_y, offset[1], offset[2]))
    face = jnp.where(on_x, 0, jnp.where(on_y, 1, 2)) * 2 + (normal > 0).astype(jnp.int32)
    cell = jnp.clip((side * (xyz - 0.3) / 0.4).astype(jnp.int32), 0, side - 1)
    code, u, v = [jnp.zeros_like(face) for _ in range(3)]
    for place, (axis, sign, corner, first) in enumerate(FACES):
        here = face == 2 * axis + sign
        second = 3 - axis - first
        along = [side - 1 - cell[w] if corner[w] else cell[w] for w in (first, second)]
        code = jnp.where(here, place * side * side, code)
        u = jnp.where(here, along[0], u)
        v = jnp.where(here, along[1], v)
    for bit in reversed(range(bits)):
        step = 1 << bit
        u_on = (u >> bit) & 1
        v_on = (v >> bit) & 1
        code = code + step * step * ((3 * u_on) ^ v_on)
        flip = (v_on == 0) & (u_on == 1)
        u, v = jnp.where(flip, side - 1 - u, u), jnp.where(flip, side - 1 - v, v)
        u, v = jnp.where(v_on == 0, v, u), jnp.where(v_on == 0, u, v)
    return code


def sorted_rank(xyz):
    count = xyz.shape[1]
    key = surface_key(xyz) * count + jnp.arange(count, dtype=jnp.int32)
    return jnp.sum((key[:, None] < key[None, :]).astype(jnp.int32), axis=0)


def pick_columns(xyz, pick):
    high = lax.reduce_precision(xyz, 8, 7)
    middle = lax.reduce_precision(xyz - high, 8, 7)
    low = xyz - high - middle
    parts = jnp.concatenate([high, middle, low], axis=0).astype(jnp.bfloat16)
    picked = jnp.dot(parts, pick, preferred_element_type=jnp.float32)
    return picked[0:3] + picked[3:6] + picked[6:9]


def with_boxes(xyz, size):
    count = xyz.shape[1]
    runs = xyz.reshape(3, count // size, size)
    boxes = jnp.concatenate([jnp.min(runs, axis=2), jnp.max(runs, axis=2)], axis=0).reshape(-1)
    row = jnp.pad(boxes, (0, count - boxes.shape[0]))
    return jnp.concatenate([xyz, row[None, :]], axis=0)


def near_groups(centre_data, node_data):
    rows, _, piece = centre_data.shape
    cols, _, nodes = node_data.shape
    boxes = piece // BOX
    groups = nodes // GROUP
    total = cols * groups
    turns = LANES // BLOCK
    centre_box = centre_data[:, 3, : 6 * boxes].reshape(rows, 6, boxes)
    node_box = node_data[:, 3, : 6 * groups].reshape(cols, 6, groups).transpose(1, 0, 2).reshape(6, total)
    apart = jnp.zeros((rows, boxes, total), jnp.float32)
    for axis in range(3):
        low = centre_box[:, axis, :, None] - node_box[None, None, 3 + axis, :]
        high = node_box[None, None, axis, :] - centre_box[:, 3 + axis, :, None]
        gap = jnp.maximum(jnp.maximum(low, high), 0.0)
        apart = apart + gap * gap
    apart = apart.reshape(rows // turns, turns, piece // LANES, turns, BLOCK // BOX, total)
    apart = jnp.min(apart, axis=(0, 4))
    turned = [jnp.roll(apart[k], -k, axis=1) for k in range(turns)]
    apart = jnp.minimum(jnp.minimum(turned[0], turned[1]), jnp.minimum(turned[2], turned[3]))
    near = apart.reshape(piece // BLOCK, total) <= RADIUS * RADIUS * 1.001
    blocks = near.shape[0]
    spans = total // LANES
    ones = near.astype(jnp.bfloat16).reshape(blocks * spans, LANES)
    lane = jnp.arange(LANES)
    upto = (lane[:, None] <= lane[None, :]).astype(jnp.bfloat16)
    within = jnp.dot(ones, upto, preferred_element_type=jnp.float32).reshape(blocks, spans, LANES)
    span_count = within[:, :, -1]
    span = jnp.arange(spans)
    ahead = jnp.sum(
        jnp.where(span[None, :, None] < span[None, None, :], span_count[:, :, None], 0.0), axis=1
    )
    place = (within + ahead[:, :, None]).reshape(blocks, total).astype(jnp.int32) - 1
    counts = place[:, -1] + 1
    place = jnp.where(near, place, -1)
    number = jnp.arange(total, dtype=jnp.int32)
    major = (place[:, :, None] // LANES == span[None, None, :]) & near[:, :, None]
    minor = place[:, :, None] % LANES == lane[None, None, :]
    digits = [jnp.where(minor, d[None, :, None], 0).astype(jnp.bfloat16) for d in (number // 64, number % 64)]
    listed = lax.dot_general(
        major.astype(jnp.bfloat16),
        jnp.concatenate(digits, axis=2),
        (((1,), (1,)), ((0,), (0,))),
        preferred_element_type=jnp.float32,
    )
    listed = (listed[:, :, :LANES] * 64.0 + listed[:, :, LANES:]).reshape(blocks, total)
    listed = jnp.pad(listed.astype(jnp.int32), ((0, 0), (0, BATCH)))
    slots = jnp.arange(total + BATCH, dtype=jnp.int32)
    return counts, jnp.where(slots[None, :] < counts[:, None], listed, total)


def interpolate(counts, lists, node_data, centre_data, coefs):
    rows, disp_rows, piece = coefs.shape
    cols, _, nodes = node_data.shape
    total = cols * nodes
    turns = LANES // BLOCK
    quads = rows // turns

    def kernel(count_ref, list_ref, node_ref, centre_ref, coef_ref, out_ref, acc_ref, row_ref, place_ref, weight_ref):
        acc_ref[total:, :] = jnp.zeros((GROUP, LANES), jnp.float32)
        for col in range(cols):

            def prepare(step, carry):
                first = pl.multiple_of(step * LANES, LANES)
                flat = node_ref[col, :, pl.ds(first, LANES)] * SCALE
                flat = jnp.concatenate([flat, flat], axis=0)
                row_ref[pl.ds(col * nodes + first, LANES), :] = flat.T
                acc_ref[pl.ds(col * nodes + first, LANES), :] = jnp.zeros((LANES, LANES), jnp.float32)
                return carry

            lax.fori_loop(0, nodes // LANES, prepare, 0)

        lane = lax.broadcasted_iota(jnp.int32, (1, LANES), 1)
        segment = lane // BLOCK

        def gather(take, block):
            value = take((-block) % turns)
            for k in range(1, turns):
                value = jnp.where(segment == k, take((k - block) % turns), value)
            return value

        for block in range(piece // BLOCK):
            lanes = slice(block // turns * LANES, (block // turns + 1) * LANES)
            for quad in range(quads):
                coef = gather(lambda k: coef_ref[turns * quad + k, :, lanes].astype(jnp.float32), block)
                weight_ref[:, quad * LANES : (quad + 1) * LANES] = coef.astype(jnp.bfloat16)
                for axis in range(3):
                    centre = gather(lambda k: centre_ref[turns * quad + k, axis : axis + 1, lanes], block)
                    place_ref[3 * quad + axis : 3 * quad + axis + 1, :] = centre * SCALE

            def batch(step, carry):
                ids = [list_ref[block, step * BATCH + i] for i in range(BATCH)]
                node = jnp.concatenate(
                    [
                        row_ref[pl.ds(pl.multiple_of(jnp.minimum(i, total // GROUP - 1) * GROUP, GROUP), GROUP), :]
                        for i in ids
                    ],
                    axis=0,
                )
                node = [jnp.broadcast_to(node[:, a : a + 1], (GROUP * BATCH, LANES)) for a in range(3)]
                part = jnp.zeros((GROUP * BATCH, disp_rows), jnp.float32)
                for pair in range(quads // 2):
                    tiles = []
                    for quad in (2 * pair, 2 * pair + 1):
                        squared = None
                        for axis in range(3):
                            difference = node[axis] - place_ref[3 * quad + axis : 3 * quad + axis + 1, :]
                            square = difference * difference
                            squared = square if squared is None else squared + square
                        scaled = squared * lax.rsqrt(jnp.maximum(squared, 1e-30))
                        remain = jnp.maximum(4.0 - scaled, 0.0)
                        remain = remain * remain
                        tiles.append((remain * remain * (scaled + 1.0)).astype(jnp.bfloat16))
                    part = part + lax.dot_general(
                        jnp.concatenate(tiles, axis=1),
                        weight_ref[:, pair * 2 * LANES : (pair + 1) * 2 * LANES],
                        (((1,), (1,)), ((), ())),
                        preferred_element_type=jnp.float32,
                    )
                for i, number in enumerate(ids):
                    start = pl.multiple_of(number * GROUP, GROUP)
                    acc_ref[pl.ds(start, GROUP), :disp_rows] += part[i * GROUP : (i + 1) * GROUP]
                return carry

            lax.fori_loop(0, (count_ref[block] + BATCH - 1) // BATCH, batch, 0)

        low_lanes = lane < LANES // 2
        for col in range(cols):

            def pack(step, carry):
                first = pl.multiple_of(step * LANES, LANES)
                low = acc_ref[pl.ds(col * nodes + first, LANES), :]
                high = acc_ref[pl.ds(col * nodes + nodes // 2 + first, LANES), :]
                both = jnp.where(low_lanes, low, pltpu.roll(high, LANES // 2, 1))
                out_ref[col, pl.ds(first, LANES), :] = (both * (1.0 / 256.0)).astype(jnp.bfloat16)
                return carry

            lax.fori_loop(0, nodes // 2 // LANES, pack, 0)

    vmem = pl.BlockSpec(memory_space=pltpu.VMEM)
    smem = pl.BlockSpec(memory_space=pltpu.SMEM)
    return pl.pallas_call(
        kernel,
        out_shape=jax.ShapeDtypeStruct((cols, nodes // 2, LANES), jnp.bfloat16),
        in_specs=[smem, smem, vmem, vmem, vmem],
        out_specs=vmem,
        scratch_shapes=[
            pltpu.VMEM((total + GROUP, LANES), jnp.float32),
            pltpu.VMEM((total, 8), jnp.float32),
            pltpu.VMEM((16, LANES), jnp.float32),
            pltpu.VMEM((disp_rows, quads * LANES), jnp.bfloat16),
        ],
        name="interpolate",
    )(counts, lists, node_data, centre_data, coefs)


def per_device(struct_disp, target, inverse, centre_xyz, node_xyz):
    rows = lax.axis_size("row")
    cols = lax.axis_size("col")
    row_block, col_block = inverse.shape
    disp_rows = struct_disp.shape[0]
    nodes = node_xyz.shape[1]
    piece = row_block // cols
    row_index = lax.axis_index("row")

    send = routed_entries(struct_disp, target, rows, cols, col_block)
    own_xyz = lax.dynamic_slice_in_dim(centre_xyz, row_index * row_block, row_block, 1)
    send, own_xyz, node_xyz = lax.optimization_barrier((send, own_xyz, node_xyz))
    recv = exchange(send, ("row", "col"))

    rank = sorted_rank(own_xyz)
    turn = (rank // BLOCK + row_index) % (LANES // BLOCK)
    centre_slot = rank // LANES * LANES + turn * BLOCK + rank % BLOCK
    order = jnp.arange(row_block, dtype=jnp.int32)
    centre_pick = (centre_slot[:, None] == order[None, :]).astype(jnp.bfloat16)
    piece_order = lax.axis_index("col") * piece + jnp.arange(piece, dtype=jnp.int32)
    piece_pick = (centre_slot[:, None] == piece_order[None, :]).astype(jnp.bfloat16)
    piece_data = with_boxes(pick_columns(own_xyz, piece_pick), BOX)
    centre_data = exchange(jnp.broadcast_to(piece_data[None], (rows, 4, piece)), "row")

    node_rank = sorted_rank(node_xyz)
    node_order = jnp.arange(nodes, dtype=jnp.int32)
    node_pick = (node_rank[:, None] == node_order[None, :]).astype(jnp.bfloat16)
    own_nodes = with_boxes(pick_columns(node_xyz, node_pick), GROUP)
    node_data = exchange(jnp.broadcast_to(own_nodes[None], (cols, 4, nodes)), "col")
    counts, lists = near_groups(centre_data, node_data)

    disp_bf = column_displacements(recv, disp_rows, rows, cols, col_block)
    partial = lax.dot_general(
        disp_bf, inverse, (((1,), (1,)), ((), ())), preferred_element_type=jnp.float32
    )
    partial = jnp.dot(partial.astype(jnp.bfloat16), centre_pick, preferred_element_type=jnp.float32)
    partial = partial.astype(jnp.bfloat16).reshape(disp_rows, cols, piece).transpose(1, 0, 2)
    coef = jnp.sum(exchange(partial, "col").astype(jnp.float32), axis=0)
    coef = lax.optimization_barrier(coef).astype(jnp.bfloat16)
    coefs = exchange(jnp.broadcast_to(coef[None], (rows,) + coef.shape), "row")

    outs = interpolate(counts, lists, node_data, centre_data, coefs)
    summed = jnp.sum(exchange(outs, "col").astype(jnp.float32), axis=0)
    ordered = jnp.concatenate([summed[:, :disp_rows], summed[:, 64 : 64 + disp_rows]], axis=0)
    return lax.dot_general(
        ordered.astype(jnp.bfloat16),
        node_pick,
        (((0,), (1,)), ((), ())),
        preferred_element_type=jnp.float32,
    )


def solution(mesh):
    placed = (
        P(None, ("row", "col")),
        P(("row", "col")),
        P("row", "col"),
        P(),
        P(None, ("row", "col")),
    )
    return jax.shard_map(
        per_device, mesh=mesh, in_specs=placed, out_specs=P(None, ("row", "col")), check_vma=False
    )
```

```python
import math

import jax
import jax.numpy as jnp
from jax import lax
from jax.experimental import pallas as pl
from jax.experimental.pallas import tpu as pltpu
from jax.sharding import PartitionSpec as P


M = 32768
CAP = 4
RADIUS = 2.0 / math.sqrt(M)
SCALE = 4.0 / RADIUS
GROUP = 8
BATCH = 32
LANES = 128
BLOCK = 32
BOX = 16
FACES = (
    (1, 0, (0, 0, 0), 0),
    (2, 0, (1, 0, 0), 0),
    (0, 0, (0, 0, 0), 1),
    (1, 1, (0, 1, 0), 0),
    (0, 1, (1, 1, 0), 2),
    (2, 1, (1, 1, 1), 0),
)


def exchange(value, axes):
    return lax.all_to_all(value, axes, split_axis=0, concat_axis=0, tiled=True)


def routed_entries(struct_disp, target, rows, cols, col_block):
    disp_rows, entries = struct_disp.shape
    owner_block = col_block // rows
    owner_col = target // col_block
    owner_row = target % col_block // owner_block
    offsets = target % owner_block
    owner = owner_row * cols + owner_col
    position = jnp.arange(entries, dtype=jnp.int32)
    earlier = (owner[:, None] == owner[None, :]) & (position[:, None] < position[None, :])
    rank = jnp.sum(earlier.astype(jnp.int32), axis=0)
    slots = rows * CAP
    slot = owner_col * slots + owner_row * CAP + rank
    pick = (jnp.arange(cols * slots, dtype=jnp.int32)[:, None] == slot[None, :]).astype(jnp.bfloat16)
    payload = jnp.concatenate(
        [
            struct_disp.astype(jnp.bfloat16),
            offsets.astype(jnp.bfloat16)[None, :],
            jnp.zeros((64 - disp_rows - 1, entries), jnp.bfloat16),
        ],
        axis=0,
    )
    packed = lax.dot_general(
        pick, payload, (((1,), (1,)), ((), ())), preferred_element_type=jnp.float32
    ).astype(jnp.bfloat16)
    packed = packed.reshape(cols, slots, 64)
    half = slots // 2
    packed = jnp.concatenate([packed[:, :half], packed[:, half:]], axis=-1)
    return jnp.broadcast_to(packed[None], (rows, cols, half, 128)).reshape(rows * cols, half, 128)


def column_displacements(recv, disp_rows, rows, cols, col_block):
    owner_block = col_block // rows
    recv = recv.reshape(rows * cols, rows // 2, CAP, 128).transpose(1, 0, 2, 3)
    recv = recv.reshape(rows // 2, rows * cols * CAP, 128)
    columns = jnp.arange(owner_block, dtype=jnp.int32).astype(jnp.bfloat16)
    halves = []
    for side in range(2):
        part = recv[:, :, side * 64 : side * 64 + 64]
        place = (part[:, :, disp_rows : disp_rows + 1] == columns[None, None, :]).astype(jnp.bfloat16)
        halves.append(
            lax.dot_general(
                part[:, :, :disp_rows],
                place,
                (((1,), (1,)), ((0,), (0,))),
                preferred_element_type=jnp.float32,
            )
        )
    summed = jnp.concatenate(halves, axis=0).astype(jnp.bfloat16)
    return summed.transpose(1, 0, 2).reshape(disp_rows, col_block)


def surface_key(xyz):
    bits = 6
    side = 1 << bits
    offset = xyz - 0.5
    size = jnp.abs(offset)
    on_x = (size[0] >= size[1]) & (size[0] >= size[2])
    on_y = jnp.logical_not(on_x) & (size[1] >= size[2])
    normal = jnp.where(on_x, offset[0], jnp.where(on_y, offset[1], offset[2]))
    face = jnp.where(on_x, 0, jnp.where(on_y, 1, 2)) * 2 + (normal > 0).astype(jnp.int32)
    cell = jnp.clip((side * (xyz - 0.3) / 0.4).astype(jnp.int32), 0, side - 1)
    code, u, v = [jnp.zeros_like(face) for _ in range(3)]
    for place, (axis, sign, corner, first) in enumerate(FACES):
        here = face == 2 * axis + sign
        second = 3 - axis - first
        along = [side - 1 - cell[w] if corner[w] else cell[w] for w in (first, second)]
        code = jnp.where(here, place * side * side, code)
        u = jnp.where(here, along[0], u)
        v = jnp.where(here, along[1], v)
    for bit in reversed(range(bits)):
        step = 1 << bit
        u_on = (u >> bit) & 1
        v_on = (v >> bit) & 1
        code = code + step * step * ((3 * u_on) ^ v_on)
        flip = (v_on == 0) & (u_on == 1)
        u, v = jnp.where(flip, side - 1 - u, u), jnp.where(flip, side - 1 - v, v)
        u, v = jnp.where(v_on == 0, v, u), jnp.where(v_on == 0, u, v)
    return code


def sorted_rank(xyz):
    count = xyz.shape[1]
    key = surface_key(xyz) * count + jnp.arange(count, dtype=jnp.int32)
    return jnp.sum((key[:, None] < key[None, :]).astype(jnp.int32), axis=0)


def pick_columns(xyz, pick):
    high = lax.reduce_precision(xyz, 8, 7)
    middle = lax.reduce_precision(xyz - high, 8, 7)
    low = xyz - high - middle
    parts = jnp.concatenate([high, middle, low], axis=0).astype(jnp.bfloat16)
    picked = jnp.dot(parts, pick, preferred_element_type=jnp.float32)
    return picked[0:3] + picked[3:6] + picked[6:9]


def with_boxes(xyz, size):
    count = xyz.shape[1]
    runs = xyz.reshape(3, count // size, size)
    boxes = jnp.concatenate([jnp.min(runs, axis=2), jnp.max(runs, axis=2)], axis=0).reshape(-1)
    row = jnp.pad(boxes, (0, count - boxes.shape[0]))
    return jnp.concatenate([xyz, row[None, :]], axis=0)


def near_groups(centre_data, node_data):
    rows, _, piece = centre_data.shape
    cols, _, nodes = node_data.shape
    boxes = piece // BOX
    groups = nodes // GROUP
    total = cols * groups
    turns = LANES // BLOCK
    centre_box = centre_data[:, 3, : 6 * boxes].reshape(rows, 6, boxes)
    node_box = node_data[:, 3, : 6 * groups].reshape(cols, 6, groups).transpose(1, 0, 2).reshape(6, total)
    apart = jnp.zeros((rows, boxes, total), jnp.float32)
    for axis in range(3):
        low = centre_box[:, axis, :, None] - node_box[None, None, 3 + axis, :]
        high = node_box[None, None, axis, :] - centre_box[:, 3 + axis, :, None]
        gap = jnp.maximum(jnp.maximum(low, high), 0.0)
        apart = apart + gap * gap
    apart = apart.reshape(rows // turns, turns, piece // LANES, turns, BLOCK // BOX, total)
    apart = jnp.min(apart, axis=(0, 4))
    turned = [jnp.roll(apart[k], -k, axis=1) for k in range(turns)]
    apart = jnp.minimum(jnp.minimum(turned[0], turned[1]), jnp.minimum(turned[2], turned[3]))
    near = apart.reshape(piece // BLOCK, total) <= RADIUS * RADIUS * 1.001
    blocks = near.shape[0]
    spans = total // LANES
    ones = near.astype(jnp.bfloat16).reshape(blocks * spans, LANES)
    lane = jnp.arange(LANES)
    upto = (lane[:, None] <= lane[None, :]).astype(jnp.bfloat16)
    within = jnp.dot(ones, upto, preferred_element_type=jnp.float32).reshape(blocks, spans, LANES)
    span_count = within[:, :, -1]
    span = jnp.arange(spans)
    ahead = jnp.sum(
        jnp.where(span[None, :, None] < span[None, None, :], span_count[:, :, None], 0.0), axis=1
    )
    place = (within + ahead[:, :, None]).reshape(blocks, total).astype(jnp.int32) - 1
    counts = place[:, -1] + 1
    place = jnp.where(near, place, -1)
    number = jnp.arange(total, dtype=jnp.int32)
    major = (place[:, :, None] // LANES == span[None, None, :]) & near[:, :, None]
    minor = place[:, :, None] % LANES == lane[None, None, :]
    digits = [jnp.where(minor, d[None, :, None], 0).astype(jnp.bfloat16) for d in (number // 64, number % 64)]
    listed = lax.dot_general(
        major.astype(jnp.bfloat16),
        jnp.concatenate(digits, axis=2),
        (((1,), (1,)), ((0,), (0,))),
        preferred_element_type=jnp.float32,
    )
    listed = (listed[:, :, :LANES] * 64.0 + listed[:, :, LANES:]).reshape(blocks, total)
    listed = jnp.pad(listed.astype(jnp.int32), ((0, 0), (0, BATCH)))
    slots = jnp.arange(total + BATCH, dtype=jnp.int32)
    return counts, jnp.where(slots[None, :] < counts[:, None], listed, total)


def interpolate(counts, lists, node_data, centre_data, coefs):
    rows, disp_rows, piece = coefs.shape
    cols, _, nodes = node_data.shape
    total = cols * nodes
    turns = LANES // BLOCK
    quads = rows // turns

    def kernel(count_ref, list_ref, node_ref, centre_ref, coef_ref, out_ref, acc_ref, row_ref, place_ref, weight_ref):
        acc_ref[total:, :] = jnp.zeros((GROUP, LANES), jnp.float32)
        for col in range(cols):

            def prepare(step, carry):
                first = pl.multiple_of(step * LANES, LANES)
                flat = node_ref[col, :, pl.ds(first, LANES)] * SCALE
                flat = jnp.concatenate([flat, flat], axis=0)
                row_ref[pl.ds(col * nodes + first, LANES), :] = flat.T
                acc_ref[pl.ds(col * nodes + first, LANES), :] = jnp.zeros((LANES, LANES), jnp.float32)
                return carry

            lax.fori_loop(0, nodes // LANES, prepare, 0)

        lane = lax.broadcasted_iota(jnp.int32, (1, LANES), 1)
        segment = lane // BLOCK

        def gather(take, block):
            value = take((-block) % turns)
            for k in range(1, turns):
                value = jnp.where(segment == k, take((k - block) % turns), value)
            return value

        for block in range(piece // BLOCK):
            lanes = slice(block // turns * LANES, (block // turns + 1) * LANES)
            for quad in range(quads):
                coef = gather(lambda k: coef_ref[turns * quad + k, :, lanes].astype(jnp.float32), block)
                weight_ref[:, quad * LANES : (quad + 1) * LANES] = coef.astype(jnp.bfloat16)
                for axis in range(3):
                    centre = gather(lambda k: centre_ref[turns * quad + k, axis : axis + 1, lanes], block)
                    place_ref[3 * quad + axis : 3 * quad + axis + 1, :] = centre * SCALE

            def batch(step, carry):
                ids = [list_ref[block, step * BATCH + i] for i in range(BATCH)]
                node = jnp.concatenate(
                    [
                        row_ref[pl.ds(pl.multiple_of(jnp.minimum(i, total // GROUP - 1) * GROUP, GROUP), GROUP), :]
                        for i in ids
                    ],
                    axis=0,
                )
                node = [jnp.broadcast_to(node[:, a : a + 1], (GROUP * BATCH, LANES)) for a in range(3)]
                part = jnp.zeros((GROUP * BATCH, disp_rows), jnp.float32)
                for pair in range(quads // 2):
                    tiles = []
                    for quad in (2 * pair, 2 * pair + 1):
                        squared = None
                        for axis in range(3):
                            difference = node[axis] - place_ref[3 * quad + axis : 3 * quad + axis + 1, :]
                            square = difference * difference
                            squared = square if squared is None else squared + square
                        scaled = squared * lax.rsqrt(jnp.maximum(squared, 1e-30))
                        remain = jnp.maximum(4.0 - scaled, 0.0)
                        remain = remain * remain
                        tiles.append((remain * remain * (scaled + 1.0)).astype(jnp.bfloat16))
                    part = part + lax.dot_general(
                        jnp.concatenate(tiles, axis=1),
                        weight_ref[:, pair * 2 * LANES : (pair + 1) * 2 * LANES],
                        (((1,), (1,)), ((), ())),
                        preferred_element_type=jnp.float32,
                    )
                for i, number in enumerate(ids):
                    start = pl.multiple_of(number * GROUP, GROUP)
                    acc_ref[pl.ds(start, GROUP), :disp_rows] += part[i * GROUP : (i + 1) * GROUP]
                return carry

            lax.fori_loop(0, (count_ref[block] + BATCH - 1) // BATCH, batch, 0)

        low_lanes = lane < LANES // 2
        for col in range(cols):

            def pack(step, carry):
                first = pl.multiple_of(step * LANES, LANES)
                low = acc_ref[pl.ds(col * nodes + first, LANES), :]
                high = acc_ref[pl.ds(col * nodes + nodes // 2 + first, LANES), :]
                both = jnp.where(low_lanes, low, pltpu.roll(high, LANES // 2, 1))
                out_ref[col, pl.ds(first, LANES), :] = (both * (1.0 / 256.0)).astype(jnp.bfloat16)
                return carry

            lax.fori_loop(0, nodes // 2 // LANES, pack, 0)

    vmem = pl.BlockSpec(memory_space=pltpu.VMEM)
    smem = pl.BlockSpec(memory_space=pltpu.SMEM)
    return pl.pallas_call(
        kernel,
        out_shape=jax.ShapeDtypeStruct((cols, nodes // 2, LANES), jnp.bfloat16),
        in_specs=[smem, smem, vmem, vmem, vmem],
        out_specs=vmem,
        scratch_shapes=[
            pltpu.VMEM((total + GROUP, LANES), jnp.float32),
            pltpu.VMEM((total, 8), jnp.float32),
            pltpu.VMEM((16, LANES), jnp.float32),
            pltpu.VMEM((disp_rows, quads * LANES), jnp.bfloat16),
        ],
        name="interpolate",
    )(counts, lists, node_data, centre_data, coefs)


def per_device(struct_disp, target, inverse, centre_xyz, node_xyz):
    rows = lax.axis_size("row")
    cols = lax.axis_size("col")
    row_block, col_block = inverse.shape
    disp_rows = struct_disp.shape[0]
    nodes = node_xyz.shape[1]
    piece = row_block // cols
    row_index = lax.axis_index("row")

    send = routed_entries(struct_disp, target, rows, cols, col_block)
    own_xyz = lax.dynamic_slice_in_dim(centre_xyz, row_index * row_block, row_block, 1)
    send, own_xyz, node_xyz = lax.optimization_barrier((send, own_xyz, node_xyz))
    recv = exchange(send, ("row", "col"))

    rank = sorted_rank(own_xyz)
    turn = (rank // BLOCK + row_index) % (LANES // BLOCK)
    centre_slot = rank // LANES * LANES + turn * BLOCK + rank % BLOCK
    order = jnp.arange(row_block, dtype=jnp.int32)
    centre_pick = (centre_slot[:, None] == order[None, :]).astype(jnp.bfloat16)
    piece_order = lax.axis_index("col") * piece + jnp.arange(piece, dtype=jnp.int32)
    piece_pick = (centre_slot[:, None] == piece_order[None, :]).astype(jnp.bfloat16)
    piece_data = with_boxes(pick_columns(own_xyz, piece_pick), BOX)
    centre_data = exchange(jnp.broadcast_to(piece_data[None], (rows, 4, piece)), "row")

    node_rank = sorted_rank(node_xyz)
    node_order = jnp.arange(nodes, dtype=jnp.int32)
    node_pick = (node_rank[:, None] == node_order[None, :]).astype(jnp.bfloat16)
    own_nodes = with_boxes(pick_columns(node_xyz, node_pick), GROUP)
    node_data = exchange(jnp.broadcast_to(own_nodes[None], (cols, 4, nodes)), "col")
    counts, lists = near_groups(centre_data, node_data)

    disp_bf = column_displacements(recv, disp_rows, rows, cols, col_block)
    partial = lax.dot_general(
        disp_bf, inverse, (((1,), (1,)), ((), ())), preferred_element_type=jnp.float32
    )
    partial = jnp.dot(partial.astype(jnp.bfloat16), centre_pick, preferred_element_type=jnp.float32)
    partial = partial.astype(jnp.bfloat16).reshape(disp_rows, cols, piece).transpose(1, 0, 2)
    partial = exchange(partial, "col")
    coef = jnp.sum(partial.astype(jnp.float32), axis=0)
    coef = lax.optimization_barrier(coef).astype(jnp.bfloat16)
    coefs = exchange(jnp.broadcast_to(coef[None], (rows,) + coef.shape), "row")

    outs = interpolate(counts, lists, node_data, centre_data, coefs)
    summed = jnp.sum(exchange(outs, "col").astype(jnp.float32), axis=0)
    ordered = jnp.concatenate([summed[:, :disp_rows], summed[:, 64 : 64 + disp_rows]], axis=0)
    return lax.dot_general(
        ordered.astype(jnp.bfloat16),
        node_pick,
        (((0,), (1,)), ((), ())),
        preferred_element_type=jnp.float32,
    )


def solution(mesh):
    placed = (
        P(None, ("row", "col")),
        P(("row", "col")),
        P("row", "col"),
        P(),
        P(None, ("row", "col")),
    )
    return jax.shard_map(per_device, mesh=mesh, in_specs=placed, out_specs=P(None, ("row", "col")), check_vma=False)
```

```python
import math

import jax
import jax.numpy as jnp
from jax import lax
from jax.experimental import pallas as pl
from jax.experimental.pallas import tpu as pltpu
from jax.sharding import PartitionSpec as P


M = 32768
CAP = 4
RADIUS = 2.0 / math.sqrt(M)
SCALE = 4.0 / RADIUS
GROUP = 8
BATCH = 32
LANES = 128
BLOCK = 32
BOX = 16
FACES = (
    (1, 0, (0, 0, 0), 0),
    (2, 0, (1, 0, 0), 0),
    (0, 0, (0, 0, 0), 1),
    (1, 1, (0, 1, 0), 0),
    (0, 1, (1, 1, 0), 2),
    (2, 1, (1, 1, 1), 0),
)


def exchange(value, axes):
    return lax.all_to_all(value, axes, split_axis=0, concat_axis=0, tiled=True)


def routed_entries(struct_disp, target, rows, cols, col_block):
    disp_rows, entries = struct_disp.shape
    owner_block = col_block // rows
    owner_col = target // col_block
    owner_row = target % col_block // owner_block
    offsets = target % owner_block
    owner = owner_row * cols + owner_col
    position = jnp.arange(entries, dtype=jnp.int32)
    earlier = (owner[:, None] == owner[None, :]) & (position[:, None] < position[None, :])
    rank = jnp.sum(earlier.astype(jnp.int32), axis=0)
    slots = rows * CAP
    slot = owner_col * slots + owner_row * CAP + rank
    pick = (jnp.arange(cols * slots, dtype=jnp.int32)[:, None] == slot[None, :]).astype(jnp.bfloat16)
    payload = jnp.concatenate(
        [
            struct_disp.astype(jnp.bfloat16),
            offsets.astype(jnp.bfloat16)[None, :],
            jnp.zeros((64 - disp_rows - 1, entries), jnp.bfloat16),
        ],
        axis=0,
    )
    packed = lax.dot_general(
        pick, payload, (((1,), (1,)), ((), ())), preferred_element_type=jnp.float32
    ).astype(jnp.bfloat16)
    packed = packed.reshape(cols, slots, 64)
    half = slots // 2
    packed = jnp.concatenate([packed[:, :half], packed[:, half:]], axis=-1)
    return jnp.broadcast_to(packed[None], (rows, cols, half, 128)).reshape(rows * cols, half, 128)


def column_displacements(recv, disp_rows, rows, cols, col_block):
    owner_block = col_block // rows
    recv = recv.reshape(rows * cols, rows // 2, CAP, 128).transpose(1, 0, 2, 3)
    recv = recv.reshape(rows // 2, rows * cols * CAP, 128)
    columns = jnp.arange(owner_block, dtype=jnp.int32).astype(jnp.bfloat16)
    halves = []
    for side in range(2):
        part = recv[:, :, side * 64 : side * 64 + 64]
        place = (part[:, :, disp_rows : disp_rows + 1] == columns[None, None, :]).astype(jnp.bfloat16)
        halves.append(
            lax.dot_general(
                part[:, :, :disp_rows],
                place,
                (((1,), (1,)), ((0,), (0,))),
                preferred_element_type=jnp.float32,
            )
        )
    summed = jnp.concatenate(halves, axis=0).astype(jnp.bfloat16)
    return summed.transpose(1, 0, 2).reshape(disp_rows, col_block)


def surface_key(xyz):
    bits = 6
    side = 1 << bits
    offset = xyz - 0.5
    size = jnp.abs(offset)
    on_x = (size[0] >= size[1]) & (size[0] >= size[2])
    on_y = jnp.logical_not(on_x) & (size[1] >= size[2])
    normal = jnp.where(on_x, offset[0], jnp.where(on_y, offset[1], offset[2]))
    face = jnp.where(on_x, 0, jnp.where(on_y, 1, 2)) * 2 + (normal > 0).astype(jnp.int32)
    cell = jnp.clip((side * (xyz - 0.3) / 0.4).astype(jnp.int32), 0, side - 1)
    code, u, v = [jnp.zeros_like(face) for _ in range(3)]
    for place, (axis, sign, corner, first) in enumerate(FACES):
        here = face == 2 * axis + sign
        second = 3 - axis - first
        along = [side - 1 - cell[w] if corner[w] else cell[w] for w in (first, second)]
        code = jnp.where(here, place * side * side, code)
        u = jnp.where(here, along[0], u)
        v = jnp.where(here, along[1], v)
    for bit in reversed(range(bits)):
        step = 1 << bit
        u_on = (u >> bit) & 1
        v_on = (v >> bit) & 1
        code = code + step * step * ((3 * u_on) ^ v_on)
        flip = (v_on == 0) & (u_on == 1)
        u, v = jnp.where(flip, side - 1 - u, u), jnp.where(flip, side - 1 - v, v)
        u, v = jnp.where(v_on == 0, v, u), jnp.where(v_on == 0, u, v)
    return code


def sorted_rank(xyz):
    count = xyz.shape[1]
    key = surface_key(xyz) * count + jnp.arange(count, dtype=jnp.int32)
    return jnp.sum((key[:, None] < key[None, :]).astype(jnp.int32), axis=0)


def pick_columns(xyz, pick):
    high = lax.reduce_precision(xyz, 8, 7)
    middle = lax.reduce_precision(xyz - high, 8, 7)
    low = xyz - high - middle
    parts = jnp.concatenate([high, middle, low], axis=0).astype(jnp.bfloat16)
    picked = jnp.dot(parts, pick, preferred_element_type=jnp.float32)
    return picked[0:3] + picked[3:6] + picked[6:9]


def with_boxes(xyz, size):
    count = xyz.shape[1]
    runs = xyz.reshape(3, count // size, size)
    boxes = jnp.concatenate([jnp.min(runs, axis=2), jnp.max(runs, axis=2)], axis=0).reshape(-1)
    row = jnp.pad(boxes, (0, count - boxes.shape[0]))
    return jnp.concatenate([xyz, row[None, :]], axis=0)


def near_groups(centre_data, node_data):
    rows, _, piece = centre_data.shape
    cols, _, nodes = node_data.shape
    boxes = piece // BOX
    groups = nodes // GROUP
    total = cols * groups
    turns = LANES // BLOCK
    centre_box = centre_data[:, 3, : 6 * boxes].reshape(rows, 6, boxes)
    node_box = node_data[:, 3, : 6 * groups].reshape(cols, 6, groups).transpose(1, 0, 2).reshape(6, total)
    apart = jnp.zeros((rows, boxes, total), jnp.float32)
    for axis in range(3):
        low = centre_box[:, axis, :, None] - node_box[None, None, 3 + axis, :]
        high = node_box[None, None, axis, :] - centre_box[:, 3 + axis, :, None]
        gap = jnp.maximum(jnp.maximum(low, high), 0.0)
        apart = apart + gap * gap
    apart = apart.reshape(rows // turns, turns, piece // LANES, turns, BLOCK // BOX, total)
    apart = jnp.min(apart, axis=(0, 4))
    turned = [jnp.roll(apart[k], -k, axis=1) for k in range(turns)]
    apart = jnp.minimum(jnp.minimum(turned[0], turned[1]), jnp.minimum(turned[2], turned[3]))
    return apart.reshape(piece // BLOCK, total) <= RADIUS * RADIUS * 1.001


def listed_groups(near):
    total = near.shape[1]
    blocks = near.shape[0]
    spans = total // LANES
    ones = near.astype(jnp.bfloat16).reshape(blocks * spans, LANES)
    lane = jnp.arange(LANES)
    upto = (lane[:, None] <= lane[None, :]).astype(jnp.bfloat16)
    within = jnp.dot(ones, upto, preferred_element_type=jnp.float32).reshape(blocks, spans, LANES)
    span_count = within[:, :, -1]
    span = jnp.arange(spans)
    ahead = jnp.sum(
        jnp.where(span[None, :, None] < span[None, None, :], span_count[:, :, None], 0.0), axis=1
    )
    place = (within + ahead[:, :, None]).reshape(blocks, total).astype(jnp.int32) - 1
    counts = place[:, -1] + 1
    place = jnp.where(near, place, -1)
    number = jnp.arange(total, dtype=jnp.int32)
    major = (place[:, :, None] // LANES == span[None, None, :]) & near[:, :, None]
    minor = place[:, :, None] % LANES == lane[None, None, :]
    digits = [jnp.where(minor, d[None, :, None], 0).astype(jnp.bfloat16) for d in (number // 64, number % 64)]
    listed = lax.dot_general(
        major.astype(jnp.bfloat16),
        jnp.concatenate(digits, axis=2),
        (((1,), (1,)), ((0,), (0,))),
        preferred_element_type=jnp.float32,
    )
    listed = (listed[:, :, :LANES] * 64.0 + listed[:, :, LANES:]).reshape(blocks, total)
    listed = jnp.pad(listed.astype(jnp.int32), ((0, 0), (0, BATCH)))
    slots = jnp.arange(total + BATCH, dtype=jnp.int32)
    return counts, jnp.where(slots[None, :] < counts[:, None], listed, total)


def interpolate(parity, counts, lists, node_data, centre_data, coefs):
    rows, disp_rows, piece = coefs.shape
    cols, _, nodes = node_data.shape
    total = cols * nodes
    last = total // GROUP
    turns = LANES // BLOCK
    quads = rows // turns
    blocks = piece // BLOCK
    size = GROUP * BATCH

    def kernel(
        parity_ref,
        count_ref,
        list_ref,
        node_ref,
        centre_ref,
        coef_ref,
        own_ref,
        other_ref,
        acc_ref,
        row_ref,
        place_ref,
        weight_ref,
        phi_0,
        phi_1,
        spread_0,
        spread_1,
        table_ref,
    ):
        acc_ref[total:, :] = jnp.zeros((GROUP, LANES), jnp.float32)
        for col in range(cols):

            def prepare(step, carry):
                first = pl.multiple_of(step * LANES, LANES)
                flat = node_ref[col, :, pl.ds(first, LANES)] * SCALE
                flat = jnp.concatenate([flat, flat], axis=0)
                row_ref[pl.ds(col * nodes + first, LANES), :] = flat.T
                acc_ref[pl.ds(col * nodes + first, LANES), :] = jnp.zeros((LANES, LANES), jnp.float32)
                return carry

            lax.fori_loop(0, nodes // LANES, prepare, 0)

        lane = lax.broadcasted_iota(jnp.int32, (1, LANES), 1)
        segment = lane // BLOCK

        def gather(take, block):
            value = take((-block) % turns)
            for k in range(1, turns):
                value = jnp.where(segment == k, take((k - block) % turns), value)
            return value

        def fill(number, block, start):
            table_ref[0, number] = block
            table_ref[1, number] = start

        fill(0, 0, last)
        number = 1
        for block in range(blocks):
            lanes = slice(block // turns * LANES, (block // turns + 1) * LANES)
            for quad in range(quads):
                coef = gather(lambda k: coef_ref[turns * quad + k, :, lanes].astype(jnp.float32), block)
                weight_ref[block, :, quad * LANES : (quad + 1) * LANES] = coef.astype(jnp.bfloat16)
                for axis in range(3):
                    centre = gather(lambda k: centre_ref[turns * quad + k, axis : axis + 1, lanes], block)
                    row = 16 * block + 3 * quad + axis
                    place_ref[row : row + 1, :] = centre * SCALE

            def add(step, place):
                fill(place, block, step * BATCH)
                return place + 1

            number = lax.fori_loop(0, (count_ref[block] + BATCH - 1) // BATCH, add, number)
        for extra in range(3):
            fill(number + extra, 0, last)

        def ids(place):
            block = table_ref[0, place]
            start = table_ref[1, place]
            return [list_ref[block, start + i] for i in range(BATCH)]

        def spread(place, spread_ref):
            node = jnp.concatenate(
                [
                    row_ref[pl.ds(pl.multiple_of(jnp.minimum(i, last - 1) * GROUP, GROUP), GROUP), :]
                    for i in ids(place)
                ],
                axis=0,
            )
            for axis in range(3):
                spread_ref[axis * size : (axis + 1) * size, :] = jnp.broadcast_to(
                    node[:, axis : axis + 1], (size, LANES)
                )

        def evaluate(place, spread_ref, phi_ref):
            block = table_ref[0, place]
            for quad in range(quads):
                squared = None
                for axis in range(3):
                    centre = place_ref[pl.ds(16 * block + 3 * quad + axis, 1), :]
                    difference = spread_ref[axis * size : (axis + 1) * size, :] - centre
                    square = difference * difference
                    squared = square if squared is None else squared + square
                scaled = squared * lax.rsqrt(jnp.maximum(squared, 1e-30))
                remain = jnp.maximum(4.0 - scaled, 0.0)
                remain = remain * remain
                phi = remain * remain * (scaled + 1.0)
                phi_ref[:, quad * LANES : (quad + 1) * LANES] = phi.astype(jnp.bfloat16)

        def collect(place, phi_ref):
            block = table_ref[0, place]
            part = lax.dot_general(
                phi_ref[...],
                weight_ref[block],
                (((1,), (1,)), ((), ())),
                preferred_element_type=jnp.float32,
            )
            for i, group in enumerate(ids(place)):
                start = pl.multiple_of(group * GROUP, GROUP)
                acc_ref[pl.ds(start, GROUP), :disp_rows] += part[i * GROUP : (i + 1) * GROUP]

        spread(1, spread_0)

        def two(step, carry):
            place = 2 * step + 1
            collect(place - 1, phi_1)
            evaluate(place, spread_0, phi_0)
            spread(place + 1, spread_1)
            collect(place, phi_0)
            evaluate(place + 1, spread_1, phi_1)
            spread(place + 2, spread_0)
            return carry

        lax.fori_loop(0, (number + 1) // 2, two, 0)

        low_lanes = lane < LANES // 2
        for side, out_ref in enumerate((own_ref, other_ref)):
            for chip in range(cols // 2):
                col = 2 * chip + (parity_ref[0] + side) % 2

                def pack(step, carry):
                    first = pl.multiple_of(step * LANES, LANES)
                    start = pl.multiple_of(col * nodes, nodes) + first
                    low = acc_ref[pl.ds(start, LANES), :]
                    high = acc_ref[pl.ds(start + nodes // 2, LANES), :]
                    both = jnp.where(low_lanes, low, pltpu.roll(high, LANES // 2, 1))
                    out_ref[chip, pl.ds(first, LANES), :] = (both * (1.0 / 256.0)).astype(jnp.bfloat16)
                    return carry

                lax.fori_loop(0, nodes // 2 // LANES, pack, 0)

    vmem = pl.BlockSpec(memory_space=pltpu.VMEM)
    smem = pl.BlockSpec(memory_space=pltpu.SMEM)
    out = jax.ShapeDtypeStruct((cols // 2, nodes // 2, LANES), jnp.bfloat16)
    return pl.pallas_call(
        kernel,
        out_shape=(out, out),
        in_specs=[smem, smem, smem, vmem, vmem, vmem],
        out_specs=(vmem, vmem),
        scratch_shapes=[
            pltpu.VMEM((total + GROUP, LANES), jnp.float32),
            pltpu.VMEM((total, 8), jnp.float32),
            pltpu.VMEM((16 * blocks, LANES), jnp.float32),
            pltpu.VMEM((blocks, disp_rows, quads * LANES), jnp.bfloat16),
            pltpu.VMEM((size, quads * LANES), jnp.bfloat16),
            pltpu.VMEM((size, quads * LANES), jnp.bfloat16),
            pltpu.VMEM((3 * size, LANES), jnp.float32),
            pltpu.VMEM((3 * size, LANES), jnp.float32),
            pltpu.SMEM((2, blocks * (last // BATCH) + 4), jnp.int32),
        ],
        name="interpolate",
    )(parity, counts, lists, node_data, centre_data, coefs)


def per_device(struct_disp, target, inverse, centre_xyz, node_xyz):
    rows = lax.axis_size("row")
    cols = lax.axis_size("col")
    row_block, col_block = inverse.shape
    disp_rows = struct_disp.shape[0]
    nodes = node_xyz.shape[1]
    piece = row_block // cols
    row_index = lax.axis_index("row")

    send = routed_entries(struct_disp, target, rows, cols, col_block)
    own_xyz = lax.dynamic_slice_in_dim(centre_xyz, row_index * row_block, row_block, 1)
    send, own_xyz, node_xyz = lax.optimization_barrier((send, own_xyz, node_xyz))
    recv = exchange(send, ("row", "col"))

    rank = sorted_rank(own_xyz)
    turn = (rank // BLOCK + row_index) % (LANES // BLOCK)
    centre_slot = rank // LANES * LANES + turn * BLOCK + rank % BLOCK
    order = jnp.arange(row_block, dtype=jnp.int32)
    centre_pick = (centre_slot[:, None] == order[None, :]).astype(jnp.bfloat16)
    piece_order = lax.axis_index("col") * piece + jnp.arange(piece, dtype=jnp.int32)
    piece_pick = (centre_slot[:, None] == piece_order[None, :]).astype(jnp.bfloat16)
    piece_data = with_boxes(pick_columns(own_xyz, piece_pick), BOX)
    centre_data = exchange(jnp.broadcast_to(piece_data[None], (rows, 4, piece)), "row")

    node_rank = sorted_rank(node_xyz)
    node_order = jnp.arange(nodes, dtype=jnp.int32)
    node_pick = (node_rank[:, None] == node_order[None, :]).astype(jnp.bfloat16)
    own_nodes = with_boxes(pick_columns(node_xyz, node_pick), GROUP)
    node_data = exchange(jnp.broadcast_to(own_nodes[None], (cols, 4, nodes)), "col")
    near = near_groups(centre_data, node_data)
    counts, lists = listed_groups(near)

    disp_bf = column_displacements(recv, disp_rows, rows, cols, col_block)
    partial = lax.dot_general(
        disp_bf, inverse, (((1,), (1,)), ((), ())), preferred_element_type=jnp.float32
    )
    partial = jnp.dot(partial.astype(jnp.bfloat16), centre_pick, preferred_element_type=jnp.float32)
    partial = partial.astype(jnp.bfloat16).reshape(disp_rows, cols, piece).transpose(1, 0, 2)
    partial = exchange(partial, "col")
    coef = jnp.sum(partial.astype(jnp.float32), axis=0)
    coef = lax.optimization_barrier(coef).astype(jnp.bfloat16)
    coefs = exchange(jnp.broadcast_to(coef[None], (rows,) + coef.shape), "row")

    parity = (lax.axis_index("col") % 2).astype(jnp.int32).reshape(1)
    own, other = interpolate(parity, counts, lists, node_data, centre_data, coefs)
    other = lax.ppermute(other, "col", [(c, c ^ 1) for c in range(cols)])
    both = (own.astype(jnp.float32) + other.astype(jnp.float32)).astype(jnp.bfloat16)
    chips = [[c for c in range(cols) if c % 2 == core] for core in range(2)]
    both = lax.all_to_all(
        both, "col", split_axis=0, concat_axis=0, axis_index_groups=chips, tiled=True
    )
    summed = jnp.sum(both.astype(jnp.float32), axis=0)
    ordered = jnp.concatenate([summed[:, :disp_rows], summed[:, 64 : 64 + disp_rows]], axis=0)
    return lax.dot_general(
        ordered.astype(jnp.bfloat16),
        node_pick,
        (((0,), (1,)), ((), ())),
        preferred_element_type=jnp.float32,
    )


def solution(mesh):
    placed = (
        P(None, ("row", "col")),
        P(("row", "col")),
        P("row", "col"),
        P(),
        P(None, ("row", "col")),
    )
    return jax.shard_map(per_device, mesh=mesh, in_specs=placed, out_specs=P(None, ("row", "col")), check_vma=False)
```

```python
import math

import jax
import jax.numpy as jnp
from jax import lax
from jax.experimental import pallas as pl
from jax.experimental.pallas import tpu as pltpu
from jax.sharding import PartitionSpec as P


M = 32768
CAP = 4
RADIUS = 2.0 / math.sqrt(M)
SCALE = 4.0 / RADIUS
GROUP = 8
BATCH = 32
LANES = 128
BLOCK = 32
BOX = 16
FACES = (
    (1, 0, (0, 0, 0), 0),
    (2, 0, (1, 0, 0), 0),
    (0, 0, (0, 0, 0), 1),
    (1, 1, (0, 1, 0), 0),
    (0, 1, (1, 1, 0), 2),
    (2, 1, (1, 1, 1), 0),
)


def exchange(value, axes):
    return lax.all_to_all(value, axes, split_axis=0, concat_axis=0, tiled=True)


def routed_entries(struct_disp, target, rows, cols, col_block):
    disp_rows, entries = struct_disp.shape
    owner_block = col_block // rows
    owner_col = target // col_block
    owner_row = target % col_block // owner_block
    offsets = target % owner_block
    owner = owner_row * cols + owner_col
    position = jnp.arange(entries, dtype=jnp.int32)
    earlier = (owner[:, None] == owner[None, :]) & (position[:, None] < position[None, :])
    rank = jnp.sum(earlier.astype(jnp.int32), axis=0)
    slots = rows * CAP
    slot = owner_col * slots + owner_row * CAP + rank
    pick = (jnp.arange(cols * slots, dtype=jnp.int32)[:, None] == slot[None, :]).astype(jnp.bfloat16)
    payload = jnp.concatenate(
        [
            struct_disp.astype(jnp.bfloat16),
            offsets.astype(jnp.bfloat16)[None, :],
            jnp.zeros((64 - disp_rows - 1, entries), jnp.bfloat16),
        ],
        axis=0,
    )
    packed = lax.dot_general(
        pick, payload, (((1,), (1,)), ((), ())), preferred_element_type=jnp.float32
    ).astype(jnp.bfloat16)
    packed = packed.reshape(cols, slots, 64)
    half = slots // 2
    packed = jnp.concatenate([packed[:, :half], packed[:, half:]], axis=-1)
    return jnp.broadcast_to(packed[None], (rows, cols, half, 128)).reshape(rows * cols, half, 128)


def column_displacements(recv, disp_rows, rows, cols, col_block):
    owner_block = col_block // rows
    recv = recv.reshape(rows * cols, rows // 2, CAP, 128).transpose(1, 0, 2, 3)
    recv = recv.reshape(rows // 2, rows * cols * CAP, 128)
    columns = jnp.arange(owner_block, dtype=jnp.int32).astype(jnp.bfloat16)
    halves = []
    for side in range(2):
        part = recv[:, :, side * 64 : side * 64 + 64]
        place = (part[:, :, disp_rows : disp_rows + 1] == columns[None, None, :]).astype(jnp.bfloat16)
        halves.append(
            lax.dot_general(
                part[:, :, :disp_rows],
                place,
                (((1,), (1,)), ((0,), (0,))),
                preferred_element_type=jnp.float32,
            )
        )
    summed = jnp.concatenate(halves, axis=0).astype(jnp.bfloat16)
    return summed.transpose(1, 0, 2).reshape(disp_rows, col_block)


def surface_key(xyz):
    bits = 6
    side = 1 << bits
    offset = xyz - 0.5
    size = jnp.abs(offset)
    on_x = (size[0] >= size[1]) & (size[0] >= size[2])
    on_y = jnp.logical_not(on_x) & (size[1] >= size[2])
    normal = jnp.where(on_x, offset[0], jnp.where(on_y, offset[1], offset[2]))
    face = jnp.where(on_x, 0, jnp.where(on_y, 1, 2)) * 2 + (normal > 0).astype(jnp.int32)
    cell = jnp.clip((side * (xyz - 0.3) / 0.4).astype(jnp.int32), 0, side - 1)
    code, u, v = [jnp.zeros_like(face) for _ in range(3)]
    for place, (axis, sign, corner, first) in enumerate(FACES):
        here = face == 2 * axis + sign
        second = 3 - axis - first
        along = [side - 1 - cell[w] if corner[w] else cell[w] for w in (first, second)]
        code = jnp.where(here, place * side * side, code)
        u = jnp.where(here, along[0], u)
        v = jnp.where(here, along[1], v)
    for bit in reversed(range(bits)):
        step = 1 << bit
        u_on = (u >> bit) & 1
        v_on = (v >> bit) & 1
        code = code + step * step * ((3 * u_on) ^ v_on)
        flip = (v_on == 0) & (u_on == 1)
        u, v = jnp.where(flip, side - 1 - u, u), jnp.where(flip, side - 1 - v, v)
        u, v = jnp.where(v_on == 0, v, u), jnp.where(v_on == 0, u, v)
    return code


def sorted_rank(xyz):
    count = xyz.shape[1]
    key = surface_key(xyz) * count + jnp.arange(count, dtype=jnp.int32)
    return jnp.sum((key[:, None] < key[None, :]).astype(jnp.int32), axis=0)


def pick_columns(xyz, pick):
    high = lax.reduce_precision(xyz, 8, 7)
    middle = lax.reduce_precision(xyz - high, 8, 7)
    low = xyz - high - middle
    parts = jnp.concatenate([high, middle, low], axis=0).astype(jnp.bfloat16)
    picked = jnp.dot(parts, pick, preferred_element_type=jnp.float32)
    return picked[0:3] + picked[3:6] + picked[6:9]


def with_boxes(xyz, size):
    count = xyz.shape[1]
    runs = xyz.reshape(3, count // size, size)
    boxes = jnp.concatenate([jnp.min(runs, axis=2), jnp.max(runs, axis=2)], axis=0).reshape(-1)
    row = jnp.pad(boxes, (0, count - boxes.shape[0]))
    return jnp.concatenate([xyz, row[None, :]], axis=0)


def near_groups(centre_data, node_data):
    rows, _, piece = centre_data.shape
    cols, _, nodes = node_data.shape
    boxes = piece // BOX
    groups = nodes // GROUP
    total = cols * groups
    turns = LANES // BLOCK
    centre_box = centre_data[:, 3, : 6 * boxes].reshape(rows, 6, boxes)
    node_box = node_data[:, 3, : 6 * groups].reshape(cols, 6, groups).transpose(1, 0, 2).reshape(6, total)
    apart = jnp.zeros((rows, boxes, total), jnp.float32)
    for axis in range(3):
        low = centre_box[:, axis, :, None] - node_box[None, None, 3 + axis, :]
        high = node_box[None, None, axis, :] - centre_box[:, 3 + axis, :, None]
        gap = jnp.maximum(jnp.maximum(low, high), 0.0)
        apart = apart + gap * gap
    apart = apart.reshape(rows // turns, turns, piece // LANES, turns, BLOCK // BOX, total)
    apart = jnp.min(apart, axis=(0, 4))
    turned = [jnp.roll(apart[k], -k, axis=1) for k in range(turns)]
    apart = jnp.minimum(jnp.minimum(turned[0], turned[1]), jnp.minimum(turned[2], turned[3]))
    return apart.reshape(piece // BLOCK, total) <= RADIUS * RADIUS * 1.001


def listed_groups(near):
    total = near.shape[1]
    blocks = near.shape[0]
    spans = total // LANES
    ones = near.astype(jnp.bfloat16).reshape(blocks * spans, LANES)
    lane = jnp.arange(LANES)
    upto = (lane[:, None] <= lane[None, :]).astype(jnp.bfloat16)
    within = jnp.dot(ones, upto, preferred_element_type=jnp.float32).reshape(blocks, spans, LANES)
    span_count = within[:, :, -1]
    span = jnp.arange(spans)
    ahead = jnp.sum(
        jnp.where(span[None, :, None] < span[None, None, :], span_count[:, :, None], 0.0), axis=1
    )
    place = (within + ahead[:, :, None]).reshape(blocks, total).astype(jnp.int32) - 1
    counts = place[:, -1] + 1
    place = jnp.where(near, place, -1)
    number = jnp.arange(total, dtype=jnp.int32)
    major = (place[:, :, None] // LANES == span[None, None, :]) & near[:, :, None]
    minor = place[:, :, None] % LANES == lane[None, None, :]
    digits = [jnp.where(minor, d[None, :, None], 0).astype(jnp.bfloat16) for d in (number // 64, number % 64)]
    listed = lax.dot_general(
        major.astype(jnp.bfloat16),
        jnp.concatenate(digits, axis=2),
        (((1,), (1,)), ((0,), (0,))),
        preferred_element_type=jnp.float32,
    )
    listed = (listed[:, :, :LANES] * 64.0 + listed[:, :, LANES:]).reshape(blocks, total)
    listed = jnp.pad(listed.astype(jnp.int32), ((0, 0), (0, BATCH)))
    slots = jnp.arange(total + BATCH, dtype=jnp.int32)
    return counts, jnp.where(slots[None, :] < counts[:, None], listed, total) * GROUP


def interpolate(parity, counts, lists, node_data, centre_data, coefs):
    rows, disp_rows, piece = coefs.shape
    cols, _, nodes = node_data.shape
    total = cols * nodes
    last = total // GROUP
    turns = LANES // BLOCK
    quads = rows // turns
    blocks = piece // BLOCK
    size = GROUP * BATCH

    def kernel(
        parity_ref,
        count_ref,
        list_ref,
        node_ref,
        centre_ref,
        coef_ref,
        own_ref,
        other_ref,
        acc_ref,
        row_ref,
        place_ref,
        weight_ref,
        phi_0,
        phi_1,
        spread_0,
        spread_1,
        table_ref,
    ):
        acc_ref[total:, :] = jnp.zeros((GROUP, LANES), jnp.float32)
        row_ref[total:, :] = jnp.zeros((GROUP, 8), jnp.float32)
        for col in range(cols):

            def prepare(step, carry):
                first = pl.multiple_of(step * LANES, LANES)
                flat = node_ref[col, :, pl.ds(first, LANES)] * SCALE
                flat = jnp.concatenate([flat, flat], axis=0)
                row_ref[pl.ds(col * nodes + first, LANES), :] = flat.T
                acc_ref[pl.ds(col * nodes + first, LANES), :] = jnp.zeros((LANES, LANES), jnp.float32)
                return carry

            lax.fori_loop(0, nodes // LANES, prepare, 0, unroll=4)

        lane = lax.broadcasted_iota(jnp.int32, (1, LANES), 1)
        segment = lane // BLOCK

        def gather(take, block):
            value = take((-block) % turns)
            for k in range(1, turns):
                value = jnp.where(segment == k, take((k - block) % turns), value)
            return value

        def fill(number, block, start):
            table_ref[0, number] = block
            table_ref[1, number] = start

        fill(0, 0, last)
        number = 1
        for block in range(blocks):
            lanes = slice(block // turns * LANES, (block // turns + 1) * LANES)
            for quad in range(quads):
                coef = gather(lambda k: coef_ref[turns * quad + k, :, lanes].astype(jnp.float32), block)
                weight_ref[block, :, quad * LANES : (quad + 1) * LANES] = coef.astype(jnp.bfloat16)
                for axis in range(3):
                    centre = gather(lambda k: centre_ref[turns * quad + k, axis : axis + 1, lanes], block)
                    row = 16 * block + 3 * quad + axis
                    place_ref[row : row + 1, :] = centre * SCALE

            def add(step, place):
                fill(place, block, step * BATCH)
                return place + 1

            number = lax.fori_loop(0, (count_ref[block] + BATCH - 1) // BATCH, add, number)
        for extra in range(3):
            fill(number + extra, 0, last)

        def starts(place):
            block = table_ref[0, place]
            start = table_ref[1, place]
            return [list_ref[block, start + i] for i in range(BATCH)]

        def spread(place, spread_ref):
            node = jnp.concatenate(
                [row_ref[pl.ds(pl.multiple_of(start, GROUP), GROUP), :] for start in starts(place)],
                axis=0,
            )
            for axis in range(3):
                spread_ref[axis * size : (axis + 1) * size, :] = jnp.broadcast_to(
                    node[:, axis : axis + 1], (size, LANES)
                )

        def evaluate(place, spread_ref, phi_ref):
            block = table_ref[0, place]
            for quad in range(quads):
                squared = None
                for axis in range(3):
                    centre = place_ref[pl.ds(16 * block + 3 * quad + axis, 1), :]
                    difference = spread_ref[axis * size : (axis + 1) * size, :] - centre
                    square = difference * difference
                    squared = square if squared is None else squared + square
                scaled = squared * lax.rsqrt(jnp.maximum(squared, 1e-30))
                remain = jnp.maximum(4.0 - scaled, 0.0)
                remain = remain * remain
                phi = remain * remain * (scaled + 1.0)
                phi_ref[:, quad * LANES : (quad + 1) * LANES] = phi.astype(jnp.bfloat16)

        def collect(place, phi_ref):
            block = table_ref[0, place]
            part = lax.dot_general(
                phi_ref[...],
                weight_ref[block],
                (((1,), (1,)), ((), ())),
                preferred_element_type=jnp.float32,
            )
            places = [pl.ds(pl.multiple_of(start, GROUP), GROUP) for start in starts(place)]
            before = [acc_ref[rows_of, :disp_rows] for rows_of in places]
            for i, rows_of in enumerate(places):
                acc_ref[rows_of, :disp_rows] = before[i] + part[i * GROUP : (i + 1) * GROUP]

        spread(1, spread_0)

        def two(step, carry):
            place = 2 * step + 1
            collect(place - 1, phi_1)
            evaluate(place, spread_0, phi_0)
            spread(place + 1, spread_1)
            collect(place, phi_0)
            evaluate(place + 1, spread_1, phi_1)
            spread(place + 2, spread_0)
            return carry

        lax.fori_loop(0, (number + 1) // 2, two, 0)

        low_lanes = lane < LANES // 2
        for side, out_ref in enumerate((own_ref, other_ref)):
            for chip in range(cols // 2):
                col = 2 * chip + (parity_ref[0] + side) % 2

                def pack(step, carry):
                    first = pl.multiple_of(step * LANES, LANES)
                    start = pl.multiple_of(col * nodes, nodes) + first
                    low = acc_ref[pl.ds(start, LANES), :]
                    high = acc_ref[pl.ds(start + nodes // 2, LANES), :]
                    both = jnp.where(low_lanes, low, pltpu.roll(high, LANES // 2, 1))
                    out_ref[chip, pl.ds(first, LANES), :] = (both * (1.0 / 256.0)).astype(jnp.bfloat16)
                    return carry

                lax.fori_loop(0, nodes // 2 // LANES, pack, 0, unroll=4)

    vmem = pl.BlockSpec(memory_space=pltpu.VMEM)
    smem = pl.BlockSpec(memory_space=pltpu.SMEM)
    out = jax.ShapeDtypeStruct((cols // 2, nodes // 2, LANES), jnp.bfloat16)
    return pl.pallas_call(
        kernel,
        out_shape=(out, out),
        in_specs=[smem, smem, smem, vmem, vmem, vmem],
        out_specs=(vmem, vmem),
        scratch_shapes=[
            pltpu.VMEM((total + GROUP, LANES), jnp.float32),
            pltpu.VMEM((total + GROUP, 8), jnp.float32),
            pltpu.VMEM((16 * blocks, LANES), jnp.float32),
            pltpu.VMEM((blocks, disp_rows, quads * LANES), jnp.bfloat16),
            pltpu.VMEM((size, quads * LANES), jnp.bfloat16),
            pltpu.VMEM((size, quads * LANES), jnp.bfloat16),
            pltpu.VMEM((3 * size, LANES), jnp.float32),
            pltpu.VMEM((3 * size, LANES), jnp.float32),
            pltpu.SMEM((2, blocks * (last // BATCH) + 4), jnp.int32),
        ],
        name="interpolate",
    )(parity, counts, lists, node_data, centre_data, coefs)


def per_device(struct_disp, target, inverse, centre_xyz, node_xyz):
    rows = lax.axis_size("row")
    cols = lax.axis_size("col")
    row_block, col_block = inverse.shape
    disp_rows = struct_disp.shape[0]
    nodes = node_xyz.shape[1]
    piece = row_block // cols
    row_index = lax.axis_index("row")

    send = routed_entries(struct_disp, target, rows, cols, col_block)
    own_xyz = lax.dynamic_slice_in_dim(centre_xyz, row_index * row_block, row_block, 1)
    send, own_xyz, node_xyz = lax.optimization_barrier((send, own_xyz, node_xyz))
    recv = exchange(send, ("row", "col"))

    rank = sorted_rank(own_xyz)
    block = rank // BLOCK
    turns = LANES // BLOCK
    place = block // cols
    centre_slot = block % cols * piece + place // turns * LANES + (place + row_index) % turns * BLOCK + rank % BLOCK
    order = jnp.arange(row_block, dtype=jnp.int32)
    centre_pick = (centre_slot[:, None] == order[None, :]).astype(jnp.bfloat16)
    piece_order = lax.axis_index("col") * piece + jnp.arange(piece, dtype=jnp.int32)
    piece_pick = (centre_slot[:, None] == piece_order[None, :]).astype(jnp.bfloat16)
    piece_data = with_boxes(pick_columns(own_xyz, piece_pick), BOX)
    centre_data = exchange(jnp.broadcast_to(piece_data[None], (rows, 4, piece)), "row")

    node_rank = sorted_rank(node_xyz)
    node_order = jnp.arange(nodes, dtype=jnp.int32)
    node_pick = (node_rank[:, None] == node_order[None, :]).astype(jnp.bfloat16)
    own_nodes = with_boxes(pick_columns(node_xyz, node_pick), GROUP)
    node_data = exchange(jnp.broadcast_to(own_nodes[None], (cols, 4, nodes)), "col")
    near = near_groups(centre_data, node_data)
    counts, lists = listed_groups(near)

    disp_bf = column_displacements(recv, disp_rows, rows, cols, col_block)
    partial = lax.dot_general(
        disp_bf, inverse, (((1,), (1,)), ((), ())), preferred_element_type=jnp.float32
    )
    partial = jnp.dot(partial.astype(jnp.bfloat16), centre_pick, preferred_element_type=jnp.float32)
    partial = partial.astype(jnp.bfloat16).reshape(disp_rows, cols, piece).transpose(1, 0, 2)
    partial = exchange(partial, "col")
    coef = jnp.sum(partial.astype(jnp.float32), axis=0)
    coef = lax.optimization_barrier(coef).astype(jnp.bfloat16)
    coefs = exchange(jnp.broadcast_to(coef[None], (rows,) + coef.shape), "row")

    parity = (lax.axis_index("col") % 2).astype(jnp.int32).reshape(1)
    own, other = interpolate(parity, counts, lists, node_data, centre_data, coefs)
    other = lax.ppermute(other, "col", [(c, c ^ 1) for c in range(cols)])
    both = (own.astype(jnp.float32) + other.astype(jnp.float32)).astype(jnp.bfloat16)
    chips = [[c for c in range(cols) if c % 2 == core] for core in range(2)]
    both = lax.all_to_all(
        both, "col", split_axis=0, concat_axis=0, axis_index_groups=chips, tiled=True
    )
    summed = jnp.sum(both.astype(jnp.float32), axis=0)
    ordered = jnp.concatenate([summed[:, :disp_rows], summed[:, 64 : 64 + disp_rows]], axis=0)
    return lax.dot_general(
        ordered.astype(jnp.bfloat16),
        node_pick,
        (((0,), (1,)), ((), ())),
        preferred_element_type=jnp.float32,
    )


def solution(mesh):
    placed = (
        P(None, ("row", "col")),
        P(("row", "col")),
        P("row", "col"),
        P(),
        P(None, ("row", "col")),
    )
    return jax.shard_map(per_device, mesh=mesh, in_specs=placed, out_specs=P(None, ("row", "col")), check_vma=False)
```

```python
import math

import jax
import jax.numpy as jnp
from jax import lax
from jax.experimental import pallas as pl
from jax.experimental.pallas import tpu as pltpu
from jax.sharding import PartitionSpec as P


M = 32768
CAP = 4
RADIUS = 2.0 / math.sqrt(M)
SCALE = 4.0 / RADIUS
GROUP = 8
BATCH = 32
LANES = 128
BLOCK = 32
BOX = 16
PARTS = 8
PACK = 64
FACES = (
    (1, 0, (0, 0, 0), 0),
    (2, 0, (1, 0, 0), 0),
    (0, 0, (0, 0, 0), 1),
    (1, 1, (0, 1, 0), 0),
    (0, 1, (1, 1, 0), 2),
    (2, 1, (1, 1, 1), 0),
)


def exchange(value, axes):
    return lax.all_to_all(value, axes, split_axis=0, concat_axis=0, tiled=True)


def routed_entries(struct_disp, target, rows, cols, col_block):
    disp_rows, entries = struct_disp.shape
    owner_block = col_block // rows
    owner_col = target // col_block
    owner_row = target % col_block // owner_block
    offsets = target % owner_block
    owner = owner_row * cols + owner_col
    position = jnp.arange(entries, dtype=jnp.int32)
    earlier = (owner[:, None] == owner[None, :]) & (position[:, None] < position[None, :])
    rank = jnp.sum(earlier.astype(jnp.int32), axis=0)
    slots = rows * CAP
    slot = owner_col * slots + owner_row * CAP + rank
    pick = (jnp.arange(cols * slots, dtype=jnp.int32)[:, None] == slot[None, :]).astype(jnp.bfloat16)
    payload = jnp.concatenate(
        [
            struct_disp.astype(jnp.bfloat16),
            offsets.astype(jnp.bfloat16)[None, :],
            jnp.zeros((64 - disp_rows - 1, entries), jnp.bfloat16),
        ],
        axis=0,
    )
    packed = lax.dot_general(
        pick, payload, (((1,), (1,)), ((), ())), preferred_element_type=jnp.float32
    ).astype(jnp.bfloat16)
    packed = packed.reshape(cols, slots, 64)
    half = slots // 2
    packed = jnp.concatenate([packed[:, :half], packed[:, half:]], axis=-1)
    return jnp.broadcast_to(packed[None], (rows, cols, half, 128)).reshape(rows * cols, half, 128)


def column_displacements(recv, disp_rows, rows, cols, col_block):
    owner_block = col_block // rows
    recv = recv.reshape(rows * cols, rows // 2, CAP, 128).transpose(1, 0, 2, 3)
    recv = recv.reshape(rows // 2, rows * cols * CAP, 128)
    columns = jnp.arange(owner_block, dtype=jnp.int32).astype(jnp.bfloat16)
    halves = []
    for side in range(2):
        part = recv[:, :, side * 64 : side * 64 + 64]
        place = (part[:, :, disp_rows : disp_rows + 1] == columns[None, None, :]).astype(jnp.bfloat16)
        halves.append(
            lax.dot_general(
                part[:, :, :disp_rows],
                place,
                (((1,), (1,)), ((0,), (0,))),
                preferred_element_type=jnp.float32,
            )
        )
    summed = jnp.concatenate(halves, axis=0).astype(jnp.bfloat16)
    return summed.transpose(1, 0, 2).reshape(disp_rows, col_block)


def surface_key(xyz):
    bits = 6
    side = 1 << bits
    offset = xyz - 0.5
    size = jnp.abs(offset)
    on_x = (size[0] >= size[1]) & (size[0] >= size[2])
    on_y = jnp.logical_not(on_x) & (size[1] >= size[2])
    normal = jnp.where(on_x, offset[0], jnp.where(on_y, offset[1], offset[2]))
    face = jnp.where(on_x, 0, jnp.where(on_y, 1, 2)) * 2 + (normal > 0).astype(jnp.int32)
    cell = jnp.clip((side * (xyz - 0.3) / 0.4).astype(jnp.int32), 0, side - 1)
    code, u, v = [jnp.zeros_like(face) for _ in range(3)]
    for place, (axis, sign, corner, first) in enumerate(FACES):
        here = face == 2 * axis + sign
        second = 3 - axis - first
        along = [side - 1 - cell[w] if corner[w] else cell[w] for w in (first, second)]
        code = jnp.where(here, place * side * side, code)
        u = jnp.where(here, along[0], u)
        v = jnp.where(here, along[1], v)
    for bit in reversed(range(bits)):
        step = 1 << bit
        u_on = (u >> bit) & 1
        v_on = (v >> bit) & 1
        code = code + step * step * ((3 * u_on) ^ v_on)
        flip = (v_on == 0) & (u_on == 1)
        u, v = jnp.where(flip, side - 1 - u, u), jnp.where(flip, side - 1 - v, v)
        u, v = jnp.where(v_on == 0, v, u), jnp.where(v_on == 0, u, v)
    return code


def sorted_rank(xyz):
    count = xyz.shape[1]
    key = surface_key(xyz) * count + jnp.arange(count, dtype=jnp.int32)
    return jnp.sum((key[:, None] < key[None, :]).astype(jnp.int32), axis=0)


def pick_columns(xyz, pick):
    high = lax.reduce_precision(xyz, 8, 7)
    middle = lax.reduce_precision(xyz - high, 8, 7)
    low = xyz - high - middle
    parts = jnp.concatenate([high, middle, low], axis=0).astype(jnp.bfloat16)
    picked = jnp.dot(parts, pick, preferred_element_type=jnp.float32)
    return picked[0:3] + picked[3:6] + picked[6:9]


def with_boxes(xyz, size):
    count = xyz.shape[1]
    runs = xyz.reshape(3, count // size, size)
    boxes = jnp.concatenate([jnp.min(runs, axis=2), jnp.max(runs, axis=2)], axis=0).reshape(-1)
    row = jnp.pad(boxes, (0, count - boxes.shape[0]))
    return jnp.concatenate([xyz, row[None, :]], axis=0)


def near_groups(centre_data, node_data):
    rows, _, piece = centre_data.shape
    cols, _, nodes = node_data.shape
    boxes = piece // BOX
    groups = nodes // GROUP
    total = cols * groups
    turns = LANES // BLOCK
    centre_box = centre_data[:, 3, : 6 * boxes].reshape(rows, 6, boxes)
    node_box = node_data[:, 3, : 6 * groups].reshape(cols, 6, groups).transpose(1, 0, 2).reshape(6, total)
    apart = jnp.zeros((rows, boxes, total), jnp.float32)
    for axis in range(3):
        low = centre_box[:, axis, :, None] - node_box[None, None, 3 + axis, :]
        high = node_box[None, None, axis, :] - centre_box[:, 3 + axis, :, None]
        gap = jnp.maximum(jnp.maximum(low, high), 0.0)
        apart = apart + gap * gap
    apart = apart.reshape(rows // turns, turns, piece // LANES, turns, BLOCK // BOX, total)
    apart = jnp.min(apart, axis=(0, 4))
    turned = [jnp.roll(apart[k], -k, axis=1) for k in range(turns)]
    apart = jnp.minimum(jnp.minimum(turned[0], turned[1]), jnp.minimum(turned[2], turned[3]))
    return apart.reshape(piece // BLOCK, total) <= RADIUS * RADIUS * 1.001


def listed_groups(near):
    total = near.shape[1]
    blocks = near.shape[0]
    spans = total // LANES
    ones = near.astype(jnp.bfloat16).reshape(blocks * spans, LANES)
    lane = jnp.arange(LANES)
    upto = (lane[:, None] <= lane[None, :]).astype(jnp.bfloat16)
    within = jnp.dot(ones, upto, preferred_element_type=jnp.float32).reshape(blocks, spans, LANES)
    span_count = within[:, :, -1]
    span = jnp.arange(spans)
    ahead = jnp.sum(
        jnp.where(span[None, :, None] < span[None, None, :], span_count[:, :, None], 0.0), axis=1
    )
    place = (within + ahead[:, :, None]).reshape(blocks, total).astype(jnp.int32) - 1
    counts = place[:, -1] + 1
    place = jnp.where(near, place, -1)
    number = jnp.arange(total, dtype=jnp.int32)
    major = (place[:, :, None] // LANES == span[None, None, :]) & near[:, :, None]
    minor = place[:, :, None] % LANES == lane[None, None, :]
    digits = [jnp.where(minor, d[None, :, None], 0).astype(jnp.bfloat16) for d in (number // 64, number % 64)]
    listed = lax.dot_general(
        major.astype(jnp.bfloat16),
        jnp.concatenate(digits, axis=2),
        (((1,), (1,)), ((0,), (0,))),
        preferred_element_type=jnp.float32,
    )
    listed = (listed[:, :, :LANES] * 64.0 + listed[:, :, LANES:]).reshape(blocks, total)
    listed = jnp.pad(listed.astype(jnp.int32), ((0, 0), (0, BATCH)))
    slots = jnp.arange(total + BATCH, dtype=jnp.int32)
    return counts, jnp.where(slots[None, :] < counts[:, None], listed, total) * GROUP


def interpolate(parity, counts, lists, node_data, centre_data, coefs):
    rows, disp_rows, piece = coefs.shape
    cols, _, nodes = node_data.shape
    total = cols * nodes
    last = total // GROUP
    turns = LANES // BLOCK
    quads = rows // turns
    blocks = piece // BLOCK
    size = GROUP * BATCH

    def kernel(
        parity_ref,
        count_ref,
        list_ref,
        node_ref,
        centre_ref,
        coef_ref,
        own_ref,
        other_ref,
        acc_ref,
        row_ref,
        place_ref,
        weight_ref,
        phi_0,
        phi_1,
        spread_0,
        spread_1,
        table_ref,
    ):
        acc_ref[total:, :] = jnp.zeros((GROUP, LANES), jnp.float32)
        row_ref[total:, :] = jnp.zeros((GROUP, 8), jnp.float32)
        for col in range(cols):

            def prepare(step, carry):
                first = pl.multiple_of(step * LANES, LANES)
                flat = node_ref[col, :, pl.ds(first, LANES)] * SCALE
                flat = jnp.concatenate([flat, flat], axis=0)
                row_ref[pl.ds(col * nodes + first, LANES), :] = flat.T
                acc_ref[pl.ds(col * nodes + first, LANES), :] = jnp.zeros((LANES, LANES), jnp.float32)
                return carry

            lax.fori_loop(0, nodes // LANES, prepare, 0, unroll=4)

        lane = lax.broadcasted_iota(jnp.int32, (1, LANES), 1)
        segment = lane // BLOCK

        def gather(take, block):
            value = take((-block) % turns)
            for k in range(1, turns):
                value = jnp.where(segment == k, take((k - block) % turns), value)
            return value

        def fill(number, block, start):
            table_ref[0, number] = block
            table_ref[1, number] = start

        fill(0, 0, last)
        number = 1
        for block in range(blocks):
            lanes = slice(block // turns * LANES, (block // turns + 1) * LANES)
            for quad in range(quads):
                coef = gather(lambda k: coef_ref[turns * quad + k, :, lanes].astype(jnp.float32), block)
                weight_ref[block, :, quad * LANES : (quad + 1) * LANES] = coef.astype(jnp.bfloat16)
                for axis in range(3):
                    centre = gather(lambda k: centre_ref[turns * quad + k, axis : axis + 1, lanes], block)
                    row = 16 * block + 3 * quad + axis
                    place_ref[row : row + 1, :] = centre * SCALE

            def add(step, place):
                fill(place, block, step * BATCH)
                return place + 1

            number = lax.fori_loop(0, (count_ref[block] + BATCH - 1) // BATCH, add, number)
        for extra in range(3):
            fill(number + extra, 0, last)

        def starts(place):
            block = table_ref[0, place]
            start = table_ref[1, place]
            return [list_ref[block, start + i] for i in range(BATCH)]

        def spread(place, spread_ref):
            node = jnp.concatenate(
                [row_ref[pl.ds(pl.multiple_of(start, GROUP), GROUP), :] for start in starts(place)],
                axis=0,
            )
            for axis in range(3):
                spread_ref[axis * size : (axis + 1) * size, :] = jnp.broadcast_to(
                    node[:, axis : axis + 1], (size, LANES)
                )

        def evaluate(place, spread_ref, phi_ref):
            block = table_ref[0, place]
            for quad in range(quads):
                squared = None
                for axis in range(3):
                    centre = place_ref[pl.ds(16 * block + 3 * quad + axis, 1), :]
                    difference = spread_ref[axis * size : (axis + 1) * size, :] - centre
                    square = difference * difference
                    squared = square if squared is None else squared + square
                scaled = squared * lax.rsqrt(jnp.maximum(squared, 1e-30))
                remain = jnp.maximum(4.0 - scaled, 0.0)
                remain = remain * remain
                phi = remain * remain * (scaled + 1.0)
                phi_ref[:, quad * LANES : (quad + 1) * LANES] = phi.astype(jnp.bfloat16)

        def collect(place, phi_ref):
            block = table_ref[0, place]
            part = lax.dot_general(
                phi_ref[...],
                weight_ref[block],
                (((1,), (1,)), ((), ())),
                preferred_element_type=jnp.float32,
            )
            places = [pl.ds(pl.multiple_of(start, GROUP), GROUP) for start in starts(place)]
            before = [acc_ref[rows_of, :disp_rows] for rows_of in places]
            for i, rows_of in enumerate(places):
                acc_ref[rows_of, :disp_rows] = before[i] + part[i * GROUP : (i + 1) * GROUP]

        spread(1, spread_0)

        def two(step, carry):
            place = 2 * step + 1
            collect(place - 1, phi_1)
            evaluate(place, spread_0, phi_0)
            spread(place + 1, spread_1)
            collect(place, phi_0)
            evaluate(place + 1, spread_1, phi_1)
            spread(place + 2, spread_0)
            return carry

        lax.fori_loop(0, (number + 1) // 2, two, 0)

        part_rows = nodes // PARTS
        for side, out_ref in enumerate((own_ref, other_ref)):
            for chip in range(cols // 2):
                col = 2 * chip + (parity_ref[0] + side) % 2

                def pack(step, carry):
                    first = pl.multiple_of(step * PACK, PACK)
                    start = pl.multiple_of(col * nodes, nodes) + first
                    filled = [None] * (PARTS * disp_rows // LANES)
                    for i in range(PARTS):
                        value = acc_ref[pl.ds(start + i * part_rows, PACK), :]
                        shift = i * disp_rows % LANES
                        if shift:
                            value = pltpu.roll(value, shift, 1)
                        tile = i * disp_rows // LANES
                        if filled[tile] is None:
                            filled[tile] = value
                        else:
                            filled[tile] = jnp.where(lane < shift, filled[tile], value)
                        if shift + disp_rows > LANES:
                            filled[tile + 1] = value
                    for tile, value in enumerate(filled):
                        out_ref[chip, pl.ds(tile * part_rows + first, PACK), :] = (
                            value * (1.0 / 256.0)
                        ).astype(jnp.bfloat16)
                    return carry

                lax.fori_loop(0, part_rows // PACK, pack, 0)

    vmem = pl.BlockSpec(memory_space=pltpu.VMEM)
    smem = pl.BlockSpec(memory_space=pltpu.SMEM)
    out = jax.ShapeDtypeStruct((cols // 2, nodes * disp_rows // LANES, LANES), jnp.bfloat16)
    return pl.pallas_call(
        kernel,
        out_shape=(out, out),
        in_specs=[smem, smem, smem, vmem, vmem, vmem],
        out_specs=(vmem, vmem),
        scratch_shapes=[
            pltpu.VMEM((total + GROUP, LANES), jnp.float32),
            pltpu.VMEM((total + GROUP, 8), jnp.float32),
            pltpu.VMEM((16 * blocks, LANES), jnp.float32),
            pltpu.VMEM((blocks, disp_rows, quads * LANES), jnp.bfloat16),
            pltpu.VMEM((size, quads * LANES), jnp.bfloat16),
            pltpu.VMEM((size, quads * LANES), jnp.bfloat16),
            pltpu.VMEM((3 * size, LANES), jnp.float32),
            pltpu.VMEM((3 * size, LANES), jnp.float32),
            pltpu.SMEM((2, blocks * (last // BATCH) + 4), jnp.int32),
        ],
        name="interpolate",
    )(parity, counts, lists, node_data, centre_data, coefs)


def restore(parts, rank, disp_rows):
    count, packed_rows, _ = parts.shape
    nodes = rank.shape[1]
    part_rows = nodes // PARTS
    tiles = packed_rows // part_rows
    width = 512

    def kernel(part_ref, rank_ref, out_ref):
        turned = []
        for tile in range(tiles):
            rows_of = slice(tile * part_rows, (tile + 1) * part_rows)
            total = part_ref[0, rows_of, :].astype(jnp.float32)
            for i in range(1, count):
                total = total + part_ref[i, rows_of, :].astype(jnp.float32)
            turned.append(total.T)
        turned = jnp.concatenate(turned, axis=0)
        left = []
        for i in range(PARTS):
            value = turned[i * disp_rows : (i + 1) * disp_rows]
            high = value.astype(jnp.bfloat16)
            low = (value - high.astype(jnp.float32)).astype(jnp.bfloat16)
            left.append(jnp.concatenate([high, low], axis=0))
        sorted_row = lax.broadcasted_iota(jnp.int32, (part_rows, width), 0)
        for first in range(0, nodes, width):
            lanes = slice(first, first + width)
            result = jnp.zeros((2 * disp_rows, width), jnp.float32)
            for i in range(PARTS):
                pick = jnp.where(rank_ref[:, lanes] - i * part_rows == sorted_row, 1.0, 0.0)
                result = result + jnp.dot(
                    left[i], pick.astype(jnp.bfloat16), preferred_element_type=jnp.float32
                )
            out_ref[:, lanes] = result[:disp_rows] + result[disp_rows:]

    vmem = pl.BlockSpec(memory_space=pltpu.VMEM)
    return pl.pallas_call(
        kernel,
        out_shape=jax.ShapeDtypeStruct((disp_rows, nodes), jnp.float32),
        in_specs=[vmem, vmem],
        out_specs=vmem,
        name="restore",
    )(parts, rank)


def per_device(struct_disp, target, inverse, centre_xyz, node_xyz):
    rows = lax.axis_size("row")
    cols = lax.axis_size("col")
    row_block, col_block = inverse.shape
    disp_rows = struct_disp.shape[0]
    nodes = node_xyz.shape[1]
    piece = row_block // cols
    row_index = lax.axis_index("row")

    send = routed_entries(struct_disp, target, rows, cols, col_block)
    own_xyz = lax.dynamic_slice_in_dim(centre_xyz, row_index * row_block, row_block, 1)
    send, own_xyz, node_xyz = lax.optimization_barrier((send, own_xyz, node_xyz))
    recv = exchange(send, ("row", "col"))

    rank = sorted_rank(own_xyz)
    block = rank // BLOCK
    turns = LANES // BLOCK
    place = block // cols
    centre_slot = block % cols * piece + place // turns * LANES + (place + row_index) % turns * BLOCK + rank % BLOCK
    order = jnp.arange(row_block, dtype=jnp.int32)
    centre_pick = (centre_slot[:, None] == order[None, :]).astype(jnp.bfloat16)
    piece_order = lax.axis_index("col") * piece + jnp.arange(piece, dtype=jnp.int32)
    piece_pick = (centre_slot[:, None] == piece_order[None, :]).astype(jnp.bfloat16)
    piece_data = with_boxes(pick_columns(own_xyz, piece_pick), BOX)
    centre_data = exchange(jnp.broadcast_to(piece_data[None], (rows, 4, piece)), "row")

    node_rank = sorted_rank(node_xyz)
    node_order = jnp.arange(nodes, dtype=jnp.int32)
    node_pick = (node_rank[:, None] == node_order[None, :]).astype(jnp.bfloat16)
    own_nodes = with_boxes(pick_columns(node_xyz, node_pick), GROUP)
    node_data = exchange(jnp.broadcast_to(own_nodes[None], (cols, 4, nodes)), "col")
    near = near_groups(centre_data, node_data)
    counts, lists = listed_groups(near)

    disp_bf = column_displacements(recv, disp_rows, rows, cols, col_block)
    partial = lax.dot_general(
        disp_bf, inverse, (((1,), (1,)), ((), ())), preferred_element_type=jnp.float32
    )
    partial = jnp.dot(partial.astype(jnp.bfloat16), centre_pick, preferred_element_type=jnp.float32)
    partial = partial.astype(jnp.bfloat16).reshape(disp_rows, cols, piece).transpose(1, 0, 2)
    partial = exchange(partial, "col")
    coef = jnp.sum(partial.astype(jnp.float32), axis=0)
    coef = lax.optimization_barrier(coef).astype(jnp.bfloat16)
    coefs = exchange(jnp.broadcast_to(coef[None], (rows,) + coef.shape), "row")

    parity = (lax.axis_index("col") % 2).astype(jnp.int32).reshape(1)
    own, other = interpolate(parity, counts, lists, node_data, centre_data, coefs)
    other = lax.ppermute(other, "col", [(c, c ^ 1) for c in range(cols)])
    both = (own.astype(jnp.float32) + other.astype(jnp.float32)).astype(jnp.bfloat16)
    chips = [[c for c in range(cols) if c % 2 == core] for core in range(2)]
    both = lax.all_to_all(
        both, "col", split_axis=0, concat_axis=0, axis_index_groups=chips, tiled=True
    )
    return restore(both, node_rank[None, :], disp_rows)


def solution(mesh):
    placed = (
        P(None, ("row", "col")),
        P(("row", "col")),
        P("row", "col"),
        P(),
        P(None, ("row", "col")),
    )
    return jax.shard_map(per_device, mesh=mesh, in_specs=placed, out_specs=P(None, ("row", "col")), check_vma=False)
```

```python
import math

import jax
import jax.numpy as jnp
from jax import lax
from jax.experimental import pallas as pl
from jax.experimental.pallas import tpu as pltpu
from jax.sharding import PartitionSpec as P


M = 32768
CAP = 4
RADIUS = 2.0 / math.sqrt(M)
SCALE = 4.0 / RADIUS
GROUP = 8
BATCH = 32
LANES = 128
BLOCK = 32
BOX = 16
PARTS = 8
PACK = 64
FACES = (
    (1, 0, (0, 0, 0), 0),
    (2, 0, (1, 0, 0), 0),
    (0, 0, (0, 0, 0), 1),
    (1, 1, (0, 1, 0), 0),
    (0, 1, (1, 1, 0), 2),
    (2, 1, (1, 1, 1), 0),
)


def exchange(value, axes):
    return lax.all_to_all(value, axes, split_axis=0, concat_axis=0, tiled=True)


def routed_entries(struct_disp, target, rows, cols, col_block):
    disp_rows, entries = struct_disp.shape
    owner_block = col_block // rows
    owner_col = target // col_block
    owner_row = target % col_block // owner_block
    offsets = target % owner_block
    owner = owner_row * cols + owner_col
    position = jnp.arange(entries, dtype=jnp.int32)
    earlier = (owner[:, None] == owner[None, :]) & (position[:, None] < position[None, :])
    rank = jnp.sum(earlier.astype(jnp.int32), axis=0)
    slots = rows * CAP
    slot = owner_col * slots + owner_row * CAP + rank
    pick = (jnp.arange(cols * slots, dtype=jnp.int32)[:, None] == slot[None, :]).astype(jnp.bfloat16)
    payload = jnp.concatenate(
        [
            struct_disp.astype(jnp.bfloat16),
            offsets.astype(jnp.bfloat16)[None, :],
            jnp.zeros((64 - disp_rows - 1, entries), jnp.bfloat16),
        ],
        axis=0,
    )
    packed = lax.dot_general(
        pick, payload, (((1,), (1,)), ((), ())), preferred_element_type=jnp.float32
    ).astype(jnp.bfloat16)
    packed = packed.reshape(cols, slots, 64)
    half = slots // 2
    packed = jnp.concatenate([packed[:, :half], packed[:, half:]], axis=-1)
    return jnp.broadcast_to(packed[None], (rows, cols, half, 128)).reshape(rows * cols, half, 128)


def column_displacements(recv, disp_rows, rows, cols, col_block):
    owner_block = col_block // rows
    recv = recv.reshape(rows * cols, rows // 2, CAP, 128).transpose(1, 0, 2, 3)
    recv = recv.reshape(rows // 2, rows * cols * CAP, 128)
    columns = jnp.arange(owner_block, dtype=jnp.int32).astype(jnp.bfloat16)
    halves = []
    for side in range(2):
        part = recv[:, :, side * 64 : side * 64 + 64]
        place = (part[:, :, disp_rows : disp_rows + 1] == columns[None, None, :]).astype(jnp.bfloat16)
        halves.append(
            lax.dot_general(
                part[:, :, :disp_rows],
                place,
                (((1,), (1,)), ((0,), (0,))),
                preferred_element_type=jnp.float32,
            )
        )
    return jnp.concatenate(halves, axis=0).astype(jnp.bfloat16)


def surface_key(xyz):
    bits = 6
    side = 1 << bits
    offset = xyz - 0.5
    size = jnp.abs(offset)
    on_x = (size[0] >= size[1]) & (size[0] >= size[2])
    on_y = jnp.logical_not(on_x) & (size[1] >= size[2])
    normal = jnp.where(on_x, offset[0], jnp.where(on_y, offset[1], offset[2]))
    face = jnp.where(on_x, 0, jnp.where(on_y, 1, 2)) * 2 + (normal > 0).astype(jnp.int32)
    cell = jnp.clip((side * (xyz - 0.3) / 0.4).astype(jnp.int32), 0, side - 1)
    code, u, v = [jnp.zeros_like(face) for _ in range(3)]
    for place, (axis, sign, corner, first) in enumerate(FACES):
        here = face == 2 * axis + sign
        second = 3 - axis - first
        along = [side - 1 - cell[w] if corner[w] else cell[w] for w in (first, second)]
        code = jnp.where(here, place * side * side, code)
        u = jnp.where(here, along[0], u)
        v = jnp.where(here, along[1], v)
    for bit in reversed(range(bits)):
        step = 1 << bit
        u_on = (u >> bit) & 1
        v_on = (v >> bit) & 1
        code = code + step * step * ((3 * u_on) ^ v_on)
        flip = (v_on == 0) & (u_on == 1)
        u, v = jnp.where(flip, side - 1 - u, u), jnp.where(flip, side - 1 - v, v)
        u, v = jnp.where(v_on == 0, v, u), jnp.where(v_on == 0, u, v)
    return code


def sorted_rank(xyz):
    count = xyz.shape[1]
    key = surface_key(xyz) * count + jnp.arange(count, dtype=jnp.int32)
    return jnp.sum((key[:, None] < key[None, :]).astype(jnp.int32), axis=0)


def pick_columns(xyz, pick):
    high = lax.reduce_precision(xyz, 8, 7)
    middle = lax.reduce_precision(xyz - high, 8, 7)
    low = xyz - high - middle
    parts = jnp.concatenate([high, middle, low], axis=0).astype(jnp.bfloat16)
    picked = jnp.dot(parts, pick, preferred_element_type=jnp.float32)
    return picked[0:3] + picked[3:6] + picked[6:9]


def with_boxes(xyz, size):
    count = xyz.shape[1]
    runs = xyz.reshape(3, count // size, size)
    boxes = jnp.concatenate([jnp.min(runs, axis=2), jnp.max(runs, axis=2)], axis=0).reshape(-1)
    row = jnp.pad(boxes, (0, count - boxes.shape[0]))
    return jnp.concatenate([xyz, row[None, :]], axis=0)


def near_groups(centre_data, node_data):
    rows, _, piece = centre_data.shape
    cols, _, nodes = node_data.shape
    boxes = piece // BOX
    groups = nodes // GROUP
    total = cols * groups
    turns = LANES // BLOCK
    centre_box = centre_data[:, 3, : 6 * boxes].reshape(rows, 6, boxes)
    node_box = node_data[:, 3, : 6 * groups].reshape(cols, 6, groups).transpose(1, 0, 2).reshape(6, total)
    apart = jnp.zeros((rows, boxes, total), jnp.float32)
    for axis in range(3):
        low = centre_box[:, axis, :, None] - node_box[None, None, 3 + axis, :]
        high = node_box[None, None, axis, :] - centre_box[:, 3 + axis, :, None]
        gap = jnp.maximum(jnp.maximum(low, high), 0.0)
        apart = apart + gap * gap
    apart = apart.reshape(rows // turns, turns, piece // LANES, turns, BLOCK // BOX, total)
    apart = jnp.min(apart, axis=(0, 4))
    turned = [jnp.roll(apart[k], -k, axis=1) for k in range(turns)]
    apart = jnp.minimum(jnp.minimum(turned[0], turned[1]), jnp.minimum(turned[2], turned[3]))
    return apart.reshape(piece // BLOCK, total) <= RADIUS * RADIUS * 1.001


def listed_groups(near):
    total = near.shape[1]
    blocks = near.shape[0]
    spans = total // LANES
    ones = near.astype(jnp.bfloat16).reshape(blocks * spans, LANES)
    lane = jnp.arange(LANES)
    upto = (lane[:, None] <= lane[None, :]).astype(jnp.bfloat16)
    within = jnp.dot(ones, upto, preferred_element_type=jnp.float32).reshape(blocks, spans, LANES)
    span_count = within[:, :, -1]
    span = jnp.arange(spans)
    ahead = jnp.sum(
        jnp.where(span[None, :, None] < span[None, None, :], span_count[:, :, None], 0.0), axis=1
    )
    place = (within + ahead[:, :, None]).reshape(blocks, total).astype(jnp.int32) - 1
    counts = place[:, -1] + 1
    place = jnp.where(near, place, -1)
    number = jnp.arange(total, dtype=jnp.int32)
    major = (place[:, :, None] // LANES == span[None, None, :]) & near[:, :, None]
    minor = place[:, :, None] % LANES == lane[None, None, :]
    digits = [jnp.where(minor, d[None, :, None], 0).astype(jnp.bfloat16) for d in (number // 64, number % 64)]
    listed = lax.dot_general(
        major.astype(jnp.bfloat16),
        jnp.concatenate(digits, axis=2),
        (((1,), (1,)), ((0,), (0,))),
        preferred_element_type=jnp.float32,
    )
    listed = (listed[:, :, :LANES] * 64.0 + listed[:, :, LANES:]).reshape(blocks, total)
    listed = jnp.pad(listed.astype(jnp.int32), ((0, 0), (0, BATCH)))
    slots = jnp.arange(total + BATCH, dtype=jnp.int32)
    return counts, jnp.where(slots[None, :] < counts[:, None], listed, total) * GROUP


def interpolate(parity, counts, lists, node_data, centre_data, coefs):
    rows, disp_rows, piece = coefs.shape
    cols, _, nodes = node_data.shape
    total = cols * nodes
    last = total // GROUP
    turns = LANES // BLOCK
    quads = rows // turns
    blocks = piece // BLOCK
    size = GROUP * BATCH

    def kernel(
        parity_ref,
        count_ref,
        list_ref,
        node_ref,
        centre_ref,
        coef_ref,
        own_ref,
        other_ref,
        acc_ref,
        row_ref,
        place_ref,
        weight_ref,
        phi_0,
        phi_1,
        spread_0,
        spread_1,
        table_ref,
    ):
        acc_ref[total:, :] = jnp.zeros((GROUP, LANES), jnp.float32)
        row_ref[total:, :] = jnp.zeros((GROUP, 8), jnp.float32)
        for col in range(cols):

            def prepare(step, carry):
                first = pl.multiple_of(step * LANES, LANES)
                flat = node_ref[col, :, pl.ds(first, LANES)] * SCALE
                flat = jnp.concatenate([flat, flat], axis=0)
                row_ref[pl.ds(col * nodes + first, LANES), :] = flat.T
                acc_ref[pl.ds(col * nodes + first, LANES), :] = jnp.zeros((LANES, LANES), jnp.float32)
                return carry

            lax.fori_loop(0, nodes // LANES, prepare, 0, unroll=4)

        lane = lax.broadcasted_iota(jnp.int32, (1, LANES), 1)
        segment = lane // BLOCK

        def gather(take, block):
            value = take((-block) % turns)
            for k in range(1, turns):
                value = jnp.where(segment == k, take((k - block) % turns), value)
            return value

        def fill(number, block, start):
            table_ref[0, number] = block
            table_ref[1, number] = start

        fill(0, 0, last)
        number = 1
        for block in range(blocks):
            lanes = slice(block // turns * LANES, (block // turns + 1) * LANES)
            for quad in range(quads):
                coef = gather(lambda k: coef_ref[turns * quad + k, :, lanes].astype(jnp.float32), block)
                weight_ref[block, :, quad * LANES : (quad + 1) * LANES] = coef.astype(jnp.bfloat16)
                for axis in range(3):
                    centre = gather(lambda k: centre_ref[turns * quad + k, axis : axis + 1, lanes], block)
                    row = 16 * block + 3 * quad + axis
                    place_ref[row : row + 1, :] = centre * SCALE

            def add(step, place):
                fill(place, block, step * BATCH)
                return place + 1

            number = lax.fori_loop(0, (count_ref[block] + BATCH - 1) // BATCH, add, number)
        for extra in range(3):
            fill(number + extra, 0, last)

        def starts(place):
            block = table_ref[0, place]
            start = table_ref[1, place]
            return [list_ref[block, start + i] for i in range(BATCH)]

        def spread(place, spread_ref):
            node = jnp.concatenate(
                [row_ref[pl.ds(pl.multiple_of(start, GROUP), GROUP), :] for start in starts(place)],
                axis=0,
            )
            for axis in range(3):
                spread_ref[axis * size : (axis + 1) * size, :] = jnp.broadcast_to(
                    node[:, axis : axis + 1], (size, LANES)
                )

        def evaluate(place, spread_ref, phi_ref):
            block = table_ref[0, place]
            for quad in range(quads):
                squared = None
                for axis in range(3):
                    centre = place_ref[pl.ds(16 * block + 3 * quad + axis, 1), :]
                    difference = spread_ref[axis * size : (axis + 1) * size, :] - centre
                    square = difference * difference
                    squared = square if squared is None else squared + square
                scaled = squared * lax.rsqrt(jnp.maximum(squared, 1e-30))
                remain = jnp.maximum(4.0 - scaled, 0.0)
                remain = remain * remain
                phi = remain * remain * (scaled + 1.0)
                phi_ref[:, quad * LANES : (quad + 1) * LANES] = phi.astype(jnp.bfloat16)

        def collect(place, phi_ref):
            block = table_ref[0, place]
            part = lax.dot_general(
                phi_ref[...],
                weight_ref[block],
                (((1,), (1,)), ((), ())),
                preferred_element_type=jnp.float32,
            )
            places = [pl.ds(pl.multiple_of(start, GROUP), GROUP) for start in starts(place)]
            before = [acc_ref[rows_of, :disp_rows] for rows_of in places]
            for i, rows_of in enumerate(places):
                acc_ref[rows_of, :disp_rows] = before[i] + part[i * GROUP : (i + 1) * GROUP]

        spread(1, spread_0)

        def two(step, carry):
            place = 2 * step + 1
            collect(place - 1, phi_1)
            evaluate(place, spread_0, phi_0)
            spread(place + 1, spread_1)
            collect(place, phi_0)
            evaluate(place + 1, spread_1, phi_1)
            spread(place + 2, spread_0)
            return carry

        lax.fori_loop(0, (number + 1) // 2, two, 0)

        part_rows = nodes // PARTS
        for side, out_ref in enumerate((own_ref, other_ref)):
            for chip in range(cols // 2):
                col = 2 * chip + (parity_ref[0] + side) % 2

                def pack(step, carry):
                    first = pl.multiple_of(step * PACK, PACK)
                    start = pl.multiple_of(col * nodes, nodes) + first
                    filled = [None] * (PARTS * disp_rows // LANES)
                    for i in range(PARTS):
                        value = acc_ref[pl.ds(start + i * part_rows, PACK), :]
                        shift = i * disp_rows % LANES
                        if shift:
                            value = pltpu.roll(value, shift, 1)
                        tile = i * disp_rows // LANES
                        if filled[tile] is None:
                            filled[tile] = value
                        else:
                            filled[tile] = jnp.where(lane < shift, filled[tile], value)
                        if shift + disp_rows > LANES:
                            filled[tile + 1] = value
                    for tile, value in enumerate(filled):
                        out_ref[chip, pl.ds(tile * part_rows + first, PACK), :] = (
                            value * (1.0 / 256.0)
                        ).astype(jnp.bfloat16)
                    return carry

                lax.fori_loop(0, part_rows // PACK, pack, 0)

    vmem = pl.BlockSpec(memory_space=pltpu.VMEM)
    smem = pl.BlockSpec(memory_space=pltpu.SMEM)
    out = jax.ShapeDtypeStruct((cols // 2, nodes * disp_rows // LANES, LANES), jnp.bfloat16)
    return pl.pallas_call(
        kernel,
        out_shape=(out, out),
        in_specs=[smem, smem, smem, vmem, vmem, vmem],
        out_specs=(vmem, vmem),
        scratch_shapes=[
            pltpu.VMEM((total + GROUP, LANES), jnp.float32),
            pltpu.VMEM((total + GROUP, 8), jnp.float32),
            pltpu.VMEM((16 * blocks, LANES), jnp.float32),
            pltpu.VMEM((blocks, disp_rows, quads * LANES), jnp.bfloat16),
            pltpu.VMEM((size, quads * LANES), jnp.bfloat16),
            pltpu.VMEM((size, quads * LANES), jnp.bfloat16),
            pltpu.VMEM((3 * size, LANES), jnp.float32),
            pltpu.VMEM((3 * size, LANES), jnp.float32),
            pltpu.SMEM((2, blocks * (last // BATCH) + 4), jnp.int32),
        ],
        name="interpolate",
    )(parity, counts, lists, node_data, centre_data, coefs)


def restore(parts, rank, disp_rows):
    count, packed_rows, _ = parts.shape
    nodes = rank.shape[1]
    part_rows = nodes // PARTS
    tiles = packed_rows // part_rows
    width = 512

    def kernel(part_ref, rank_ref, out_ref):
        turned = []
        for tile in range(tiles):
            rows_of = slice(tile * part_rows, (tile + 1) * part_rows)
            total = part_ref[0, rows_of, :].astype(jnp.float32)
            for i in range(1, count):
                total = total + part_ref[i, rows_of, :].astype(jnp.float32)
            turned.append(total.T)
        turned = jnp.concatenate(turned, axis=0)
        left = []
        for i in range(PARTS):
            value = turned[i * disp_rows : (i + 1) * disp_rows]
            high = value.astype(jnp.bfloat16)
            low = (value - high.astype(jnp.float32)).astype(jnp.bfloat16)
            left.append(jnp.concatenate([high, low], axis=0))
        sorted_row = lax.broadcasted_iota(jnp.int32, (part_rows, width), 0)
        for first in range(0, nodes, width):
            lanes = slice(first, first + width)
            result = jnp.zeros((2 * disp_rows, width), jnp.float32)
            for i in range(PARTS):
                pick = jnp.where(rank_ref[:, lanes] - i * part_rows == sorted_row, 1.0, 0.0)
                result = result + jnp.dot(
                    left[i], pick.astype(jnp.bfloat16), preferred_element_type=jnp.float32
                )
            out_ref[:, lanes] = result[:disp_rows] + result[disp_rows:]

    vmem = pl.BlockSpec(memory_space=pltpu.VMEM)
    return pl.pallas_call(
        kernel,
        out_shape=jax.ShapeDtypeStruct((disp_rows, nodes), jnp.float32),
        in_specs=[vmem, vmem],
        out_specs=vmem,
        name="restore",
    )(parts, rank)


def invert(disp, inverse, slot, cols):
    spans, disp_rows, width = disp.shape
    row_block, col_block = inverse.shape
    piece = row_block // cols

    def kernel(disp_ref, inverse_ref, slot_ref, out_ref, part_ref):
        step = pl.program_id(0)
        total = jnp.zeros((disp_rows, piece), jnp.float32)
        for span in range(spans):
            total = total + lax.dot_general(
                disp_ref[span],
                inverse_ref[:, span * width : (span + 1) * width],
                (((1,), (1,)), ((), ())),
                preferred_element_type=jnp.float32,
            )
        part_ref[:, pl.ds(pl.multiple_of(step * piece, piece), piece)] = total.astype(jnp.bfloat16)

        @pl.when(step == cols - 1)
        def _():
            place = lax.broadcasted_iota(jnp.int32, (piece, row_block), 0)
            for col in range(cols):
                pick = jnp.where(slot_ref[...] - col * piece == place, 1.0, 0.0).astype(jnp.bfloat16)
                moved = lax.dot_general(
                    part_ref[...], pick, (((1,), (1,)), ((), ())), preferred_element_type=jnp.float32
                )
                out_ref[col] = moved.astype(jnp.bfloat16)

    whole = lambda *shape: pl.BlockSpec(shape, lambda i: (0,) * len(shape))
    return pl.pallas_call(
        kernel,
        grid=(cols,),
        out_shape=jax.ShapeDtypeStruct((cols, disp_rows, piece), jnp.bfloat16),
        in_specs=[
            whole(spans, disp_rows, width),
            pl.BlockSpec((piece, col_block), lambda i: (i, 0)),
            whole(1, row_block),
        ],
        out_specs=whole(cols, disp_rows, piece),
        scratch_shapes=[pltpu.VMEM((disp_rows, row_block), jnp.bfloat16)],
        name="invert",
    )(disp, inverse, slot[None, :])


def per_device(struct_disp, target, inverse, centre_xyz, node_xyz):
    rows = lax.axis_size("row")
    cols = lax.axis_size("col")
    row_block, col_block = inverse.shape
    disp_rows = struct_disp.shape[0]
    nodes = node_xyz.shape[1]
    piece = row_block // cols
    row_index = lax.axis_index("row")

    send = routed_entries(struct_disp, target, rows, cols, col_block)
    own_xyz = lax.dynamic_slice_in_dim(centre_xyz, row_index * row_block, row_block, 1)
    send, own_xyz, node_xyz = lax.optimization_barrier((send, own_xyz, node_xyz))
    recv = exchange(send, ("row", "col"))

    rank = sorted_rank(own_xyz)
    block = rank // BLOCK
    turns = LANES // BLOCK
    place = block // cols
    centre_slot = block % cols * piece + place // turns * LANES + (place + row_index) % turns * BLOCK + rank % BLOCK
    piece_order = lax.axis_index("col") * piece + jnp.arange(piece, dtype=jnp.int32)
    piece_pick = (centre_slot[:, None] == piece_order[None, :]).astype(jnp.bfloat16)
    piece_data = with_boxes(pick_columns(own_xyz, piece_pick), BOX)
    centre_data = exchange(jnp.broadcast_to(piece_data[None], (rows, 4, piece)), "row")

    node_rank = sorted_rank(node_xyz)
    node_order = jnp.arange(nodes, dtype=jnp.int32)
    node_pick = (node_rank[:, None] == node_order[None, :]).astype(jnp.bfloat16)
    own_nodes = with_boxes(pick_columns(node_xyz, node_pick), GROUP)
    node_data = exchange(jnp.broadcast_to(own_nodes[None], (cols, 4, nodes)), "col")
    near = near_groups(centre_data, node_data)
    counts, lists = listed_groups(near)

    disp_bf = column_displacements(recv, disp_rows, rows, cols, col_block)
    partial = invert(disp_bf, inverse, centre_slot, cols)
    partial = exchange(partial, "col")
    coef = jnp.sum(partial.astype(jnp.float32), axis=0)
    coef = lax.optimization_barrier(coef).astype(jnp.bfloat16)
    coefs = exchange(jnp.broadcast_to(coef[None], (rows,) + coef.shape), "row")

    parity = (lax.axis_index("col") % 2).astype(jnp.int32).reshape(1)
    own, other = interpolate(parity, counts, lists, node_data, centre_data, coefs)
    other = lax.ppermute(other, "col", [(c, c ^ 1) for c in range(cols)])
    both = (own.astype(jnp.float32) + other.astype(jnp.float32)).astype(jnp.bfloat16)
    chips = [[c for c in range(cols) if c % 2 == core] for core in range(2)]
    both = lax.all_to_all(
        both, "col", split_axis=0, concat_axis=0, axis_index_groups=chips, tiled=True
    )
    return restore(both, node_rank[None, :], disp_rows)


def solution(mesh):
    placed = (
        P(None, ("row", "col")),
        P(("row", "col")),
        P("row", "col"),
        P(),
        P(None, ("row", "col")),
    )
    return jax.shard_map(per_device, mesh=mesh, in_specs=placed, out_specs=P(None, ("row", "col")), check_vma=False)
```

```python
import math

import jax
import jax.numpy as jnp
from jax import lax
from jax.experimental import pallas as pl
from jax.experimental.pallas import tpu as pltpu
from jax.sharding import PartitionSpec as P


M = 32768
CAP = 4
RADIUS = 2.0 / math.sqrt(M)
SCALE = 4.0 / RADIUS
GROUP = 8
BATCH = 32
LANES = 128
BLOCK = 32
BOX = 16
PARTS = 8
PACK = 64
FACES = (
    (1, 0, (0, 0, 0), 0),
    (2, 0, (1, 0, 0), 0),
    (0, 0, (0, 0, 0), 1),
    (1, 1, (0, 1, 0), 0),
    (0, 1, (1, 1, 0), 2),
    (2, 1, (1, 1, 1), 0),
)


def exchange(value, axes):
    return lax.all_to_all(value, axes, split_axis=0, concat_axis=0, tiled=True)


def routed_entries(struct_disp, target, rows, cols, col_block):
    disp_rows, entries = struct_disp.shape
    owner_block = col_block // rows
    owner_col = target // col_block
    owner_row = target % col_block // owner_block
    offsets = target % owner_block
    owner = owner_row * cols + owner_col
    position = jnp.arange(entries, dtype=jnp.int32)
    earlier = (owner[:, None] == owner[None, :]) & (position[:, None] < position[None, :])
    rank = jnp.sum(earlier.astype(jnp.int32), axis=0)
    slots = rows * CAP
    slot = owner_col * slots + owner_row * CAP + rank
    pick = (jnp.arange(cols * slots, dtype=jnp.int32)[:, None] == slot[None, :]).astype(jnp.bfloat16)
    payload = jnp.concatenate(
        [
            struct_disp.astype(jnp.bfloat16),
            offsets.astype(jnp.bfloat16)[None, :],
            jnp.zeros((64 - disp_rows - 1, entries), jnp.bfloat16),
        ],
        axis=0,
    )
    packed = lax.dot_general(
        pick, payload, (((1,), (1,)), ((), ())), preferred_element_type=jnp.float32
    ).astype(jnp.bfloat16)
    packed = packed.reshape(cols, slots, 64)
    half = slots // 2
    packed = jnp.concatenate([packed[:, :half], packed[:, half:]], axis=-1)
    return jnp.broadcast_to(packed[None], (rows, cols, half, 128)).reshape(rows * cols, half, 128)


def column_displacements(recv, disp_rows, rows, owner_block):
    sources, half, _ = recv.shape
    pair = 2 * CAP
    count = sources * pair

    def kernel(recv_ref, out_ref):
        column = lax.broadcasted_iota(jnp.int32, (count, 2 * owner_block), 1).astype(jnp.float32)
        row = lax.broadcasted_iota(jnp.int32, (count, 1), 0)
        second = jnp.where(row % pair >= CAP, float(owner_block), 0.0)
        for first in range(0, half, 2 * pair):
            block = recv_ref[:, first : first + 2 * pair, :].astype(jnp.float32)
            for part in range(2):
                entries = block[:, part * pair : (part + 1) * pair, :].reshape(count, LANES)
                turned = entries.T.astype(jnp.bfloat16)
                for side in range(2):
                    lane = side * (LANES // 2)
                    offset = entries[:, lane + disp_rows : lane + disp_rows + 1] + second
                    place = jnp.where(offset == column, 1.0, 0.0).astype(jnp.bfloat16)
                    moved = jnp.dot(
                        turned[lane : lane + disp_rows], place, preferred_element_type=jnp.float32
                    ).astype(jnp.bfloat16)
                    owner = side * (rows // 2) + (first // pair + part) * 2
                    out_ref[:, owner * owner_block : (owner + 2) * owner_block] = moved

    vmem = pl.BlockSpec(memory_space=pltpu.VMEM)
    return pl.pallas_call(
        kernel,
        out_shape=jax.ShapeDtypeStruct((disp_rows, rows * owner_block), jnp.bfloat16),
        in_specs=[vmem],
        out_specs=vmem,
        name="unpack",
    )(recv)


def surface_key(xyz):
    bits = 6
    side = 1 << bits
    offset = xyz - 0.5
    size = jnp.abs(offset)
    on_x = (size[0] >= size[1]) & (size[0] >= size[2])
    on_y = jnp.logical_not(on_x) & (size[1] >= size[2])
    normal = jnp.where(on_x, offset[0], jnp.where(on_y, offset[1], offset[2]))
    face = jnp.where(on_x, 0, jnp.where(on_y, 1, 2)) * 2 + (normal > 0).astype(jnp.int32)
    cell = jnp.clip((side * (xyz - 0.3) / 0.4).astype(jnp.int32), 0, side - 1)
    code, u, v = [jnp.zeros_like(face) for _ in range(3)]
    for place, (axis, sign, corner, first) in enumerate(FACES):
        here = face == 2 * axis + sign
        second = 3 - axis - first
        along = [side - 1 - cell[w] if corner[w] else cell[w] for w in (first, second)]
        code = jnp.where(here, place * side * side, code)
        u = jnp.where(here, along[0], u)
        v = jnp.where(here, along[1], v)
    for bit in reversed(range(bits)):
        step = 1 << bit
        u_on = (u >> bit) & 1
        v_on = (v >> bit) & 1
        code = code + step * step * ((3 * u_on) ^ v_on)
        flip = (v_on == 0) & (u_on == 1)
        u, v = jnp.where(flip, side - 1 - u, u), jnp.where(flip, side - 1 - v, v)
        u, v = jnp.where(v_on == 0, v, u), jnp.where(v_on == 0, u, v)
    return code


def sorted_rank(xyz):
    count = xyz.shape[1]
    key = surface_key(xyz) * count + jnp.arange(count, dtype=jnp.int32)
    return jnp.sum((key[:, None] < key[None, :]).astype(jnp.int32), axis=0)


def pick_columns(xyz, pick):
    high = lax.reduce_precision(xyz, 8, 7)
    middle = lax.reduce_precision(xyz - high, 8, 7)
    low = xyz - high - middle
    parts = jnp.concatenate([high, middle, low], axis=0).astype(jnp.bfloat16)
    picked = jnp.dot(parts, pick, preferred_element_type=jnp.float32)
    return picked[0:3] + picked[3:6] + picked[6:9]


def with_boxes(xyz, size):
    count = xyz.shape[1]
    runs = xyz.reshape(3, count // size, size)
    boxes = jnp.concatenate([jnp.min(runs, axis=2), jnp.max(runs, axis=2)], axis=0).reshape(-1)
    row = jnp.pad(boxes, (0, count - boxes.shape[0]))
    return jnp.concatenate([xyz, row[None, :]], axis=0)


def near_groups(centre_data, node_data):
    rows, _, piece = centre_data.shape
    cols, _, nodes = node_data.shape
    boxes = piece // BOX
    groups = nodes // GROUP
    total = cols * groups
    turns = LANES // BLOCK
    centre_box = centre_data[:, 3, : 6 * boxes].reshape(rows, 6, boxes)
    node_box = node_data[:, 3, : 6 * groups].reshape(cols, 6, groups).transpose(1, 0, 2).reshape(6, total)
    apart = jnp.zeros((rows, boxes, total), jnp.float32)
    for axis in range(3):
        low = centre_box[:, axis, :, None] - node_box[None, None, 3 + axis, :]
        high = node_box[None, None, axis, :] - centre_box[:, 3 + axis, :, None]
        gap = jnp.maximum(jnp.maximum(low, high), 0.0)
        apart = apart + gap * gap
    apart = apart.reshape(rows // turns, turns, piece // LANES, turns, BLOCK // BOX, total)
    apart = jnp.min(apart, axis=(0, 4))
    turned = [jnp.roll(apart[k], -k, axis=1) for k in range(turns)]
    apart = jnp.minimum(jnp.minimum(turned[0], turned[1]), jnp.minimum(turned[2], turned[3]))
    return apart.reshape(piece // BLOCK, total) <= RADIUS * RADIUS * 1.001


def listed_groups(near):
    total = near.shape[1]
    blocks = near.shape[0]
    spans = total // LANES
    ones = near.astype(jnp.bfloat16).reshape(blocks * spans, LANES)
    lane = jnp.arange(LANES)
    upto = (lane[:, None] <= lane[None, :]).astype(jnp.bfloat16)
    within = jnp.dot(ones, upto, preferred_element_type=jnp.float32).reshape(blocks, spans, LANES)
    span_count = within[:, :, -1]
    span = jnp.arange(spans)
    ahead = jnp.sum(
        jnp.where(span[None, :, None] < span[None, None, :], span_count[:, :, None], 0.0), axis=1
    )
    place = (within + ahead[:, :, None]).reshape(blocks, total).astype(jnp.int32) - 1
    counts = place[:, -1] + 1
    place = jnp.where(near, place, -1)
    number = jnp.arange(total, dtype=jnp.int32)
    major = (place[:, :, None] // LANES == span[None, None, :]) & near[:, :, None]
    minor = place[:, :, None] % LANES == lane[None, None, :]
    digits = [jnp.where(minor, d[None, :, None], 0).astype(jnp.bfloat16) for d in (number // 64, number % 64)]
    listed = lax.dot_general(
        major.astype(jnp.bfloat16),
        jnp.concatenate(digits, axis=2),
        (((1,), (1,)), ((0,), (0,))),
        preferred_element_type=jnp.float32,
    )
    listed = (listed[:, :, :LANES] * 64.0 + listed[:, :, LANES:]).reshape(blocks, total)
    listed = jnp.pad(listed.astype(jnp.int32), ((0, 0), (0, BATCH)))
    slots = jnp.arange(total + BATCH, dtype=jnp.int32)
    return counts, jnp.where(slots[None, :] < counts[:, None], listed, total) * GROUP


def interpolate(parity, counts, lists, node_data, centre_data, coefs):
    rows, disp_rows, piece = coefs.shape
    cols, _, nodes = node_data.shape
    total = cols * nodes
    last = total // GROUP
    turns = LANES // BLOCK
    quads = rows // turns
    blocks = piece // BLOCK
    size = GROUP * BATCH

    def kernel(
        parity_ref,
        count_ref,
        list_ref,
        node_ref,
        centre_ref,
        coef_ref,
        own_ref,
        other_ref,
        acc_ref,
        row_ref,
        place_ref,
        weight_ref,
        phi_0,
        phi_1,
        spread_0,
        spread_1,
        table_ref,
    ):
        acc_ref[total:, :] = jnp.zeros((GROUP, LANES), jnp.float32)
        row_ref[total:, :] = jnp.zeros((GROUP, 8), jnp.float32)
        for col in range(cols):

            def prepare(step, carry):
                first = pl.multiple_of(step * LANES, LANES)
                flat = node_ref[col, :, pl.ds(first, LANES)] * SCALE
                flat = jnp.concatenate([flat, flat], axis=0)
                row_ref[pl.ds(col * nodes + first, LANES), :] = flat.T
                acc_ref[pl.ds(col * nodes + first, LANES), :] = jnp.zeros((LANES, LANES), jnp.float32)
                return carry

            lax.fori_loop(0, nodes // LANES, prepare, 0, unroll=4)

        lane = lax.broadcasted_iota(jnp.int32, (1, LANES), 1)
        segment = lane // BLOCK

        def gather(take, block):
            value = take((-block) % turns)
            for k in range(1, turns):
                value = jnp.where(segment == k, take((k - block) % turns), value)
            return value

        def fill(number, block, start):
            table_ref[0, number] = block
            table_ref[1, number] = start

        fill(0, 0, last)
        number = 1
        for block in range(blocks):
            lanes = slice(block // turns * LANES, (block // turns + 1) * LANES)
            for quad in range(quads):
                coef = gather(lambda k: coef_ref[turns * quad + k, :, lanes].astype(jnp.float32), block)
                weight_ref[block, :, quad * LANES : (quad + 1) * LANES] = coef.astype(jnp.bfloat16)
                for axis in range(3):
                    centre = gather(lambda k: centre_ref[turns * quad + k, axis : axis + 1, lanes], block)
                    row = 16 * block + 3 * quad + axis
                    place_ref[row : row + 1, :] = centre * SCALE

            def add(step, place):
                fill(place, block, step * BATCH)
                return place + 1

            number = lax.fori_loop(0, (count_ref[block] + BATCH - 1) // BATCH, add, number)
        for extra in range(3):
            fill(number + extra, 0, last)

        def starts(place):
            block = table_ref[0, place]
            start = table_ref[1, place]
            return [list_ref[block, start + i] for i in range(BATCH)]

        def spread(place, spread_ref):
            node = jnp.concatenate(
                [row_ref[pl.ds(pl.multiple_of(start, GROUP), GROUP), :] for start in starts(place)],
                axis=0,
            )
            for axis in range(3):
                spread_ref[axis * size : (axis + 1) * size, :] = jnp.broadcast_to(
                    node[:, axis : axis + 1], (size, LANES)
                )

        def evaluate(place, spread_ref, phi_ref):
            block = table_ref[0, place]
            for quad in range(quads):
                squared = None
                for axis in range(3):
                    centre = place_ref[pl.ds(16 * block + 3 * quad + axis, 1), :]
                    difference = spread_ref[axis * size : (axis + 1) * size, :] - centre
                    square = difference * difference
                    squared = square if squared is None else squared + square
                scaled = squared * lax.rsqrt(jnp.maximum(squared, 1e-30))
                remain = jnp.maximum(4.0 - scaled, 0.0)
                remain = remain * remain
                phi = remain * remain * (scaled + 1.0)
                phi_ref[:, quad * LANES : (quad + 1) * LANES] = phi.astype(jnp.bfloat16)

        def collect(place, phi_ref):
            block = table_ref[0, place]
            part = lax.dot_general(
                phi_ref[...],
                weight_ref[block],
                (((1,), (1,)), ((), ())),
                preferred_element_type=jnp.float32,
            )
            places = [pl.ds(pl.multiple_of(start, GROUP), GROUP) for start in starts(place)]
            before = [acc_ref[rows_of, :disp_rows] for rows_of in places]
            for i, rows_of in enumerate(places):
                acc_ref[rows_of, :disp_rows] = before[i] + part[i * GROUP : (i + 1) * GROUP]

        spread(1, spread_0)

        def two(step, carry):
            place = 2 * step + 1
            collect(place - 1, phi_1)
            evaluate(place, spread_0, phi_0)
            spread(place + 1, spread_1)
            collect(place, phi_0)
            evaluate(place + 1, spread_1, phi_1)
            spread(place + 2, spread_0)
            return carry

        lax.fori_loop(0, (number + 1) // 2, two, 0)

        part_rows = nodes // PARTS
        for side, out_ref in enumerate((own_ref, other_ref)):
            for chip in range(cols // 2):
                col = 2 * chip + (parity_ref[0] + side) % 2

                def pack(step, carry):
                    first = pl.multiple_of(step * PACK, PACK)
                    start = pl.multiple_of(col * nodes, nodes) + first
                    filled = [None] * (PARTS * disp_rows // LANES)
                    for i in range(PARTS):
                        value = acc_ref[pl.ds(start + i * part_rows, PACK), :]
                        shift = i * disp_rows % LANES
                        if shift:
                            value = pltpu.roll(value, shift, 1)
                        tile = i * disp_rows // LANES
                        if filled[tile] is None:
                            filled[tile] = value
                        else:
                            filled[tile] = jnp.where(lane < shift, filled[tile], value)
                        if shift + disp_rows > LANES:
                            filled[tile + 1] = value
                    for tile, value in enumerate(filled):
                        out_ref[chip, pl.ds(tile * part_rows + first, PACK), :] = (
                            value * (1.0 / 256.0)
                        ).astype(jnp.bfloat16)
                    return carry

                lax.fori_loop(0, part_rows // PACK, pack, 0)

    vmem = pl.BlockSpec(memory_space=pltpu.VMEM)
    smem = pl.BlockSpec(memory_space=pltpu.SMEM)
    out = jax.ShapeDtypeStruct((cols // 2, nodes * disp_rows // LANES, LANES), jnp.bfloat16)
    return pl.pallas_call(
        kernel,
        out_shape=(out, out),
        in_specs=[smem, smem, smem, vmem, vmem, vmem],
        out_specs=(vmem, vmem),
        scratch_shapes=[
            pltpu.VMEM((total + GROUP, LANES), jnp.float32),
            pltpu.VMEM((total + GROUP, 8), jnp.float32),
            pltpu.VMEM((16 * blocks, LANES), jnp.float32),
            pltpu.VMEM((blocks, disp_rows, quads * LANES), jnp.bfloat16),
            pltpu.VMEM((size, quads * LANES), jnp.bfloat16),
            pltpu.VMEM((size, quads * LANES), jnp.bfloat16),
            pltpu.VMEM((3 * size, LANES), jnp.float32),
            pltpu.VMEM((3 * size, LANES), jnp.float32),
            pltpu.SMEM((2, blocks * (last // BATCH) + 4), jnp.int32),
        ],
        name="interpolate",
    )(parity, counts, lists, node_data, centre_data, coefs)


def restore(parts, rank, disp_rows):
    count, packed_rows, _ = parts.shape
    nodes = rank.shape[1]
    part_rows = nodes // PARTS
    tiles = packed_rows // part_rows
    width = 512

    def kernel(part_ref, rank_ref, out_ref):
        turned = []
        for tile in range(tiles):
            rows_of = slice(tile * part_rows, (tile + 1) * part_rows)
            total = part_ref[0, rows_of, :].astype(jnp.float32)
            for i in range(1, count):
                total = total + part_ref[i, rows_of, :].astype(jnp.float32)
            turned.append(total.T)
        turned = jnp.concatenate(turned, axis=0)
        left = []
        for i in range(PARTS):
            value = turned[i * disp_rows : (i + 1) * disp_rows]
            high = value.astype(jnp.bfloat16)
            low = (value - high.astype(jnp.float32)).astype(jnp.bfloat16)
            left.append(jnp.concatenate([high, low], axis=0))
        sorted_row = lax.broadcasted_iota(jnp.int32, (part_rows, width), 0)
        for first in range(0, nodes, width):
            lanes = slice(first, first + width)
            result = jnp.zeros((2 * disp_rows, width), jnp.float32)
            for i in range(PARTS):
                pick = jnp.where(rank_ref[:, lanes] - i * part_rows == sorted_row, 1.0, 0.0)
                result = result + jnp.dot(
                    left[i], pick.astype(jnp.bfloat16), preferred_element_type=jnp.float32
                )
            out_ref[:, lanes] = result[:disp_rows] + result[disp_rows:]

    vmem = pl.BlockSpec(memory_space=pltpu.VMEM)
    return pl.pallas_call(
        kernel,
        out_shape=jax.ShapeDtypeStruct((disp_rows, nodes), jnp.float32),
        in_specs=[vmem, vmem],
        out_specs=vmem,
        name="restore",
    )(parts, rank)


def per_device(struct_disp, target, inverse, centre_xyz, node_xyz):
    rows = lax.axis_size("row")
    cols = lax.axis_size("col")
    row_block, col_block = inverse.shape
    disp_rows = struct_disp.shape[0]
    nodes = node_xyz.shape[1]
    piece = row_block // cols
    row_index = lax.axis_index("row")

    send = routed_entries(struct_disp, target, rows, cols, col_block)
    own_xyz = lax.dynamic_slice_in_dim(centre_xyz, row_index * row_block, row_block, 1)
    send, own_xyz, node_xyz = lax.optimization_barrier((send, own_xyz, node_xyz))
    recv = exchange(send, ("row", "col"))

    rank = sorted_rank(own_xyz)
    block = rank // BLOCK
    turns = LANES // BLOCK
    place = block // cols
    centre_slot = block % cols * piece + place // turns * LANES + (place + row_index) % turns * BLOCK + rank % BLOCK
    order = jnp.arange(row_block, dtype=jnp.int32)
    centre_pick = (centre_slot[:, None] == order[None, :]).astype(jnp.bfloat16)
    piece_order = lax.axis_index("col") * piece + jnp.arange(piece, dtype=jnp.int32)
    piece_pick = (centre_slot[:, None] == piece_order[None, :]).astype(jnp.bfloat16)
    piece_data = with_boxes(pick_columns(own_xyz, piece_pick), BOX)
    centre_data = exchange(jnp.broadcast_to(piece_data[None], (rows, 4, piece)), "row")

    node_rank = sorted_rank(node_xyz)
    node_order = jnp.arange(nodes, dtype=jnp.int32)
    node_pick = (node_rank[:, None] == node_order[None, :]).astype(jnp.bfloat16)
    own_nodes = with_boxes(pick_columns(node_xyz, node_pick), GROUP)
    node_data = exchange(jnp.broadcast_to(own_nodes[None], (cols, 4, nodes)), "col")
    near = near_groups(centre_data, node_data)
    counts, lists = listed_groups(near)

    disp_bf = column_displacements(recv, disp_rows, rows, col_block // rows)
    partial = lax.dot_general(
        disp_bf, inverse, (((1,), (1,)), ((), ())), preferred_element_type=jnp.float32
    )
    partial = jnp.dot(partial.astype(jnp.bfloat16), centre_pick, preferred_element_type=jnp.float32)
    partial = partial.astype(jnp.bfloat16).reshape(disp_rows, cols, piece).transpose(1, 0, 2)
    partial = exchange(partial, "col")
    coef = jnp.sum(partial.astype(jnp.float32), axis=0)
    coef = lax.optimization_barrier(coef).astype(jnp.bfloat16)
    coefs = exchange(jnp.broadcast_to(coef[None], (rows,) + coef.shape), "row")

    parity = (lax.axis_index("col") % 2).astype(jnp.int32).reshape(1)
    own, other = interpolate(parity, counts, lists, node_data, centre_data, coefs)
    other = lax.ppermute(other, "col", [(c, c ^ 1) for c in range(cols)])
    both = (own.astype(jnp.float32) + other.astype(jnp.float32)).astype(jnp.bfloat16)
    chips = [[c for c in range(cols) if c % 2 == core] for core in range(2)]
    both = lax.all_to_all(
        both, "col", split_axis=0, concat_axis=0, axis_index_groups=chips, tiled=True
    )
    return restore(both, node_rank[None, :], disp_rows)


def solution(mesh):
    placed = (
        P(None, ("row", "col")),
        P(("row", "col")),
        P("row", "col"),
        P(),
        P(None, ("row", "col")),
    )
    return jax.shard_map(per_device, mesh=mesh, in_specs=placed, out_specs=P(None, ("row", "col")), check_vma=False)
```

```python
import math

import jax
import jax.numpy as jnp
from jax import lax
from jax.experimental import pallas as pl
from jax.experimental.pallas import tpu as pltpu
from jax.sharding import PartitionSpec as P


M = 32768
CAP = 4
RADIUS = 2.0 / math.sqrt(M)
SCALE = 4.0 / RADIUS
GROUP = 8
BATCH = 32
LANES = 128
BLOCK = 32
BOX = 16
PARTS = 8
PACK = 256
FACES = (
    (1, 0, (0, 0, 0), 0),
    (2, 0, (1, 0, 0), 0),
    (0, 0, (0, 0, 0), 1),
    (1, 1, (0, 1, 0), 0),
    (0, 1, (1, 1, 0), 2),
    (2, 1, (1, 1, 1), 0),
)


def exchange(value, axes):
    return lax.all_to_all(value, axes, split_axis=0, concat_axis=0, tiled=True)


def routed_entries(struct_disp, target, rows, cols, col_block):
    disp_rows, entries = struct_disp.shape
    owner_block = col_block // rows
    owner_col = target // col_block
    owner_row = target % col_block // owner_block
    offsets = target % owner_block
    owner = owner_row * cols + owner_col
    position = jnp.arange(entries, dtype=jnp.int32)
    earlier = (owner[:, None] == owner[None, :]) & (position[:, None] < position[None, :])
    rank = jnp.sum(earlier.astype(jnp.int32), axis=0)
    slots = rows * CAP
    slot = owner_col * slots + owner_row * CAP + rank
    pick = (jnp.arange(cols * slots, dtype=jnp.int32)[:, None] == slot[None, :]).astype(jnp.bfloat16)
    payload = jnp.concatenate(
        [
            struct_disp.astype(jnp.bfloat16),
            offsets.astype(jnp.bfloat16)[None, :],
            jnp.zeros((64 - disp_rows - 1, entries), jnp.bfloat16),
        ],
        axis=0,
    )
    packed = lax.dot_general(
        pick, payload, (((1,), (1,)), ((), ())), preferred_element_type=jnp.float32
    ).astype(jnp.bfloat16)
    packed = packed.reshape(cols, slots, 64)
    half = slots // 2
    packed = jnp.concatenate([packed[:, :half], packed[:, half:]], axis=-1)
    return jnp.broadcast_to(packed[None], (rows, cols, half, 128)).reshape(rows * cols, half, 128)


def column_displacements(recv, disp_rows, rows, owner_block):
    sources, half, _ = recv.shape
    pair = 2 * CAP
    count = sources * pair

    def kernel(recv_ref, out_ref):
        column = lax.broadcasted_iota(jnp.int32, (count, 2 * owner_block), 1).astype(jnp.float32)
        row = lax.broadcasted_iota(jnp.int32, (count, 1), 0)
        second = jnp.where(row % pair >= CAP, float(owner_block), 0.0)
        for first in range(0, half, 2 * pair):
            block = recv_ref[:, first : first + 2 * pair, :].astype(jnp.float32)
            for part in range(2):
                entries = block[:, part * pair : (part + 1) * pair, :].reshape(count, LANES)
                turned = entries.T.astype(jnp.bfloat16)
                for side in range(2):
                    lane = side * (LANES // 2)
                    offset = entries[:, lane + disp_rows : lane + disp_rows + 1] + second
                    place = jnp.where(offset == column, 1.0, 0.0).astype(jnp.bfloat16)
                    moved = jnp.dot(
                        turned[lane : lane + disp_rows], place, preferred_element_type=jnp.float32
                    ).astype(jnp.bfloat16)
                    owner = side * (rows // 2) + (first // pair + part) * 2
                    out_ref[:, owner * owner_block : (owner + 2) * owner_block] = moved

    vmem = pl.BlockSpec(memory_space=pltpu.VMEM)
    return pl.pallas_call(
        kernel,
        out_shape=jax.ShapeDtypeStruct((disp_rows, rows * owner_block), jnp.bfloat16),
        in_specs=[vmem],
        out_specs=vmem,
        name="unpack",
    )(recv)


def surface_key(xyz):
    bits = 6
    side = 1 << bits
    offset = xyz - 0.5
    size = jnp.abs(offset)
    on_x = (size[0] >= size[1]) & (size[0] >= size[2])
    on_y = jnp.logical_not(on_x) & (size[1] >= size[2])
    normal = jnp.where(on_x, offset[0], jnp.where(on_y, offset[1], offset[2]))
    face = jnp.where(on_x, 0, jnp.where(on_y, 1, 2)) * 2 + (normal > 0).astype(jnp.int32)
    cell = jnp.clip((side * (xyz - 0.3) / 0.4).astype(jnp.int32), 0, side - 1)
    code, u, v = [jnp.zeros_like(face) for _ in range(3)]
    for place, (axis, sign, corner, first) in enumerate(FACES):
        here = face == 2 * axis + sign
        second = 3 - axis - first
        along = [side - 1 - cell[w] if corner[w] else cell[w] for w in (first, second)]
        code = jnp.where(here, place * side * side, code)
        u = jnp.where(here, along[0], u)
        v = jnp.where(here, along[1], v)
    for bit in reversed(range(bits)):
        step = 1 << bit
        u_on = (u >> bit) & 1
        v_on = (v >> bit) & 1
        code = code + step * step * ((3 * u_on) ^ v_on)
        flip = (v_on == 0) & (u_on == 1)
        u, v = jnp.where(flip, side - 1 - u, u), jnp.where(flip, side - 1 - v, v)
        u, v = jnp.where(v_on == 0, v, u), jnp.where(v_on == 0, u, v)
    return code


def sorted_rank(xyz):
    count = xyz.shape[1]
    key = surface_key(xyz) * count + jnp.arange(count, dtype=jnp.int32)
    return jnp.sum((key[:, None] < key[None, :]).astype(jnp.int32), axis=0)


def pick_columns(xyz, pick):
    high = lax.reduce_precision(xyz, 8, 7)
    middle = lax.reduce_precision(xyz - high, 8, 7)
    low = xyz - high - middle
    parts = jnp.concatenate([high, middle, low], axis=0).astype(jnp.bfloat16)
    picked = jnp.dot(parts, pick, preferred_element_type=jnp.float32)
    return picked[0:3] + picked[3:6] + picked[6:9]


def with_boxes(xyz, size):
    count = xyz.shape[1]
    runs = xyz.reshape(3, count // size, size)
    boxes = jnp.concatenate([jnp.min(runs, axis=2), jnp.max(runs, axis=2)], axis=0).reshape(-1)
    row = jnp.pad(boxes, (0, count - boxes.shape[0]))
    return jnp.concatenate([xyz, row[None, :]], axis=0)


def near_groups(centre_data, node_data):
    rows, _, piece = centre_data.shape
    cols, _, nodes = node_data.shape
    boxes = piece // BOX
    groups = nodes // GROUP
    total = cols * groups
    turns = LANES // BLOCK
    centre_box = centre_data[:, 3, : 6 * boxes].reshape(rows, 6, boxes)
    node_box = node_data[:, 3, : 6 * groups].reshape(cols, 6, groups).transpose(1, 0, 2).reshape(6, total)
    apart = jnp.zeros((rows, boxes, total), jnp.float32)
    for axis in range(3):
        low = centre_box[:, axis, :, None] - node_box[None, None, 3 + axis, :]
        high = node_box[None, None, axis, :] - centre_box[:, 3 + axis, :, None]
        gap = jnp.maximum(jnp.maximum(low, high), 0.0)
        apart = apart + gap * gap
    apart = apart.reshape(rows // turns, turns, piece // LANES, turns, BLOCK // BOX, total)
    apart = jnp.min(apart, axis=(0, 4))
    turned = [jnp.roll(apart[k], -k, axis=1) for k in range(turns)]
    apart = jnp.minimum(jnp.minimum(turned[0], turned[1]), jnp.minimum(turned[2], turned[3]))
    return apart.reshape(piece // BLOCK, total) <= RADIUS * RADIUS * 1.001


def listed_groups(near):
    total = near.shape[1]
    blocks = near.shape[0]
    spans = total // LANES
    ones = near.astype(jnp.bfloat16).reshape(blocks * spans, LANES)
    lane = jnp.arange(LANES)
    upto = (lane[:, None] <= lane[None, :]).astype(jnp.bfloat16)
    within = jnp.dot(ones, upto, preferred_element_type=jnp.float32).reshape(blocks, spans, LANES)
    span_count = within[:, :, -1]
    span = jnp.arange(spans)
    ahead = jnp.sum(
        jnp.where(span[None, :, None] < span[None, None, :], span_count[:, :, None], 0.0), axis=1
    )
    place = (within + ahead[:, :, None]).reshape(blocks, total).astype(jnp.int32) - 1
    counts = place[:, -1] + 1
    place = jnp.where(near, place, -1)
    number = jnp.arange(total, dtype=jnp.int32)
    major = (place[:, :, None] // LANES == span[None, None, :]) & near[:, :, None]
    minor = place[:, :, None] % LANES == lane[None, None, :]
    digits = [jnp.where(minor, d[None, :, None], 0).astype(jnp.bfloat16) for d in (number // 64, number % 64)]
    listed = lax.dot_general(
        major.astype(jnp.bfloat16),
        jnp.concatenate(digits, axis=2),
        (((1,), (1,)), ((0,), (0,))),
        preferred_element_type=jnp.float32,
    )
    listed = (listed[:, :, :LANES] * 64.0 + listed[:, :, LANES:]).reshape(blocks, total)
    listed = jnp.pad(listed.astype(jnp.int32), ((0, 0), (0, BATCH)))
    slots = jnp.arange(total + BATCH, dtype=jnp.int32)
    return counts, jnp.where(slots[None, :] < counts[:, None], listed, total) * GROUP


def interpolate(parity, counts, lists, node_data, centre_data, coefs):
    rows, disp_rows, piece = coefs.shape
    cols, _, nodes = node_data.shape
    total = cols * nodes
    last = total // GROUP
    turns = LANES // BLOCK
    quads = rows // turns
    blocks = piece // BLOCK
    size = GROUP * BATCH

    def kernel(
        parity_ref,
        count_ref,
        list_ref,
        node_ref,
        centre_ref,
        coef_ref,
        own_ref,
        other_ref,
        acc_ref,
        row_ref,
        place_ref,
        weight_ref,
        phi_0,
        phi_1,
        spread_0,
        spread_1,
        table_ref,
    ):
        acc_ref[total:, :] = jnp.zeros((GROUP, LANES), jnp.float32)
        row_ref[total:, :] = jnp.zeros((GROUP, 8), jnp.float32)
        for col in range(cols):

            def prepare(step, carry):
                first = pl.multiple_of(step * LANES, LANES)
                flat = node_ref[col, :, pl.ds(first, LANES)] * SCALE
                flat = jnp.concatenate([flat, flat], axis=0)
                row_ref[pl.ds(col * nodes + first, LANES), :] = flat.T
                acc_ref[pl.ds(col * nodes + first, LANES), :] = jnp.zeros((LANES, LANES), jnp.float32)
                return carry

            lax.fori_loop(0, nodes // LANES, prepare, 0, unroll=16)

        lane = lax.broadcasted_iota(jnp.int32, (1, LANES), 1)
        segment = lane // BLOCK

        def gather(take, block):
            value = take((-block) % turns)
            for k in range(1, turns):
                value = jnp.where(segment == k, take((k - block) % turns), value)
            return value

        def fill(number, block, start):
            table_ref[0, number] = block
            table_ref[1, number] = start

        fill(0, 0, last)
        number = 1
        for block in range(blocks):
            lanes = slice(block // turns * LANES, (block // turns + 1) * LANES)
            for quad in range(quads):
                coef = gather(lambda k: coef_ref[turns * quad + k, :, lanes].astype(jnp.float32), block)
                weight_ref[block, :, quad * LANES : (quad + 1) * LANES] = coef.astype(jnp.bfloat16)
                for axis in range(3):
                    centre = gather(lambda k: centre_ref[turns * quad + k, axis : axis + 1, lanes], block)
                    row = 16 * block + 3 * quad + axis
                    place_ref[row : row + 1, :] = centre * SCALE

            def add(step, place):
                fill(place, block, step * BATCH)
                return place + 1

            number = lax.fori_loop(0, (count_ref[block] + BATCH - 1) // BATCH, add, number)
        for extra in range(3):
            fill(number + extra, 0, last)

        def starts(place):
            block = table_ref[0, place]
            start = table_ref[1, place]
            return [list_ref[block, start + i] for i in range(BATCH)]

        def spread(place, spread_ref):
            node = jnp.concatenate(
                [row_ref[pl.ds(pl.multiple_of(start, GROUP), GROUP), :] for start in starts(place)],
                axis=0,
            )
            for axis in range(3):
                spread_ref[axis * size : (axis + 1) * size, :] = jnp.broadcast_to(
                    node[:, axis : axis + 1], (size, LANES)
                )

        def evaluate(place, spread_ref, phi_ref):
            block = table_ref[0, place]
            for quad in range(quads):
                squared = None
                for axis in range(3):
                    centre = place_ref[pl.ds(16 * block + 3 * quad + axis, 1), :]
                    difference = spread_ref[axis * size : (axis + 1) * size, :] - centre
                    square = difference * difference
                    squared = square if squared is None else squared + square
                scaled = squared * lax.rsqrt(jnp.maximum(squared, 1e-30))
                remain = jnp.maximum(4.0 - scaled, 0.0)
                remain = remain * remain
                phi = remain * remain * (scaled + 1.0)
                phi_ref[:, quad * LANES : (quad + 1) * LANES] = phi.astype(jnp.bfloat16)

        def collect(place, phi_ref):
            block = table_ref[0, place]
            part = lax.dot_general(
                phi_ref[...],
                weight_ref[block],
                (((1,), (1,)), ((), ())),
                preferred_element_type=jnp.float32,
            )
            places = [pl.ds(pl.multiple_of(start, GROUP), GROUP) for start in starts(place)]
            for first in range(0, BATCH, 8):
                before = [acc_ref[places[i], :disp_rows] for i in range(first, first + 8)]
                for i in range(first, first + 8):
                    moved = part[i * GROUP : (i + 1) * GROUP]
                    acc_ref[places[i], :disp_rows] = before[i - first] + moved

        spread(1, spread_0)

        def two(step, carry):
            place = 2 * step + 1
            collect(place - 1, phi_1)
            evaluate(place, spread_0, phi_0)
            spread(place + 1, spread_1)
            collect(place, phi_0)
            evaluate(place + 1, spread_1, phi_1)
            spread(place + 2, spread_0)
            return carry

        lax.fori_loop(0, (number + 1) // 2, two, 0)

        part_rows = nodes // PARTS
        for side, out_ref in enumerate((own_ref, other_ref)):
            for chip in range(cols // 2):
                col = 2 * chip + (parity_ref[0] + side) % 2

                def pack(step, carry):
                    first = pl.multiple_of(step * PACK, PACK)
                    start = pl.multiple_of(col * nodes, nodes) + first
                    filled = [None] * (PARTS * disp_rows // LANES)
                    for i in range(PARTS):
                        value = acc_ref[pl.ds(start + i * part_rows, PACK), :]
                        shift = i * disp_rows % LANES
                        if shift:
                            value = pltpu.roll(value, shift, 1)
                        tile = i * disp_rows // LANES
                        if filled[tile] is None:
                            filled[tile] = value
                        else:
                            filled[tile] = jnp.where(lane < shift, filled[tile], value)
                        if shift + disp_rows > LANES:
                            filled[tile + 1] = value
                    for tile, value in enumerate(filled):
                        out_ref[chip, pl.ds(tile * part_rows + first, PACK), :] = (
                            value * (1.0 / 256.0)
                        ).astype(jnp.bfloat16)
                    return carry

                lax.fori_loop(0, part_rows // PACK, pack, 0)

    vmem = pl.BlockSpec(memory_space=pltpu.VMEM)
    smem = pl.BlockSpec(memory_space=pltpu.SMEM)
    out = jax.ShapeDtypeStruct((cols // 2, nodes * disp_rows // LANES, LANES), jnp.bfloat16)
    return pl.pallas_call(
        kernel,
        out_shape=(out, out),
        in_specs=[smem, smem, smem, vmem, vmem, vmem],
        out_specs=(vmem, vmem),
        scratch_shapes=[
            pltpu.VMEM((total + GROUP, LANES), jnp.float32),
            pltpu.VMEM((total + GROUP, 8), jnp.float32),
            pltpu.VMEM((16 * blocks, LANES), jnp.float32),
            pltpu.VMEM((blocks, disp_rows, quads * LANES), jnp.bfloat16),
            pltpu.VMEM((size, quads * LANES), jnp.bfloat16),
            pltpu.VMEM((size, quads * LANES), jnp.bfloat16),
            pltpu.VMEM((3 * size, LANES), jnp.float32),
            pltpu.VMEM((3 * size, LANES), jnp.float32),
            pltpu.SMEM((2, blocks * (last // BATCH) + 4), jnp.int32),
        ],
        name="interpolate",
    )(parity, counts, lists, node_data, centre_data, coefs)


def restore(parts, rank, disp_rows):
    count, packed_rows, _ = parts.shape
    nodes = rank.shape[1]
    part_rows = nodes // PARTS
    tiles = packed_rows // part_rows
    width = 512

    def kernel(part_ref, rank_ref, out_ref):
        turned = []
        for tile in range(tiles):
            rows_of = slice(tile * part_rows, (tile + 1) * part_rows)
            total = part_ref[0, rows_of, :].astype(jnp.float32)
            for i in range(1, count):
                total = total + part_ref[i, rows_of, :].astype(jnp.float32)
            turned.append(total.T)
        turned = jnp.concatenate(turned, axis=0)
        left = []
        for i in range(PARTS):
            value = turned[i * disp_rows : (i + 1) * disp_rows]
            high = value.astype(jnp.bfloat16)
            low = (value - high.astype(jnp.float32)).astype(jnp.bfloat16)
            left.append(jnp.concatenate([high, low], axis=0))
        sorted_row = lax.broadcasted_iota(jnp.int32, (part_rows, width), 0)
        for first in range(0, nodes, width):
            lanes = slice(first, first + width)
            result = jnp.zeros((2 * disp_rows, width), jnp.float32)
            for i in range(PARTS):
                pick = jnp.where(rank_ref[:, lanes] - i * part_rows == sorted_row, 1.0, 0.0)
                result = result + jnp.dot(
                    left[i], pick.astype(jnp.bfloat16), preferred_element_type=jnp.float32
                )
            out_ref[:, lanes] = result[:disp_rows] + result[disp_rows:]

    vmem = pl.BlockSpec(memory_space=pltpu.VMEM)
    return pl.pallas_call(
        kernel,
        out_shape=jax.ShapeDtypeStruct((disp_rows, nodes), jnp.float32),
        in_specs=[vmem, vmem],
        out_specs=vmem,
        name="restore",
    )(parts, rank)


def per_device(struct_disp, target, inverse, centre_xyz, node_xyz):
    rows = lax.axis_size("row")
    cols = lax.axis_size("col")
    row_block, col_block = inverse.shape
    disp_rows = struct_disp.shape[0]
    nodes = node_xyz.shape[1]
    piece = row_block // cols
    row_index = lax.axis_index("row")

    send = routed_entries(struct_disp, target, rows, cols, col_block)
    own_xyz = lax.dynamic_slice_in_dim(centre_xyz, row_index * row_block, row_block, 1)
    send, own_xyz, node_xyz = lax.optimization_barrier((send, own_xyz, node_xyz))
    recv = exchange(send, ("row", "col"))

    rank = sorted_rank(own_xyz)
    block = rank // BLOCK
    turns = LANES // BLOCK
    place = block // cols
    centre_slot = block % cols * piece + place // turns * LANES + (place + row_index) % turns * BLOCK + rank % BLOCK
    order = jnp.arange(row_block, dtype=jnp.int32)
    centre_pick = (centre_slot[:, None] == order[None, :]).astype(jnp.bfloat16)
    piece_order = lax.axis_index("col") * piece + jnp.arange(piece, dtype=jnp.int32)
    piece_pick = (centre_slot[:, None] == piece_order[None, :]).astype(jnp.bfloat16)
    piece_data = with_boxes(pick_columns(own_xyz, piece_pick), BOX)
    centre_data = exchange(jnp.broadcast_to(piece_data[None], (rows, 4, piece)), "row")

    node_rank = sorted_rank(node_xyz)
    node_order = jnp.arange(nodes, dtype=jnp.int32)
    node_pick = (node_rank[:, None] == node_order[None, :]).astype(jnp.bfloat16)
    own_nodes = with_boxes(pick_columns(node_xyz, node_pick), GROUP)
    node_data = exchange(jnp.broadcast_to(own_nodes[None], (cols, 4, nodes)), "col")
    near = near_groups(centre_data, node_data)
    counts, lists = listed_groups(near)

    disp_bf = column_displacements(recv, disp_rows, rows, col_block // rows)
    partial = lax.dot_general(
        disp_bf, inverse, (((1,), (1,)), ((), ())), preferred_element_type=jnp.float32
    )
    partial = jnp.dot(partial.astype(jnp.bfloat16), centre_pick, preferred_element_type=jnp.float32)
    partial = partial.astype(jnp.bfloat16).reshape(disp_rows, cols, piece).transpose(1, 0, 2)
    partial = exchange(partial, "col")
    coef = jnp.sum(partial.astype(jnp.float32), axis=0)
    coef = lax.optimization_barrier(coef).astype(jnp.bfloat16)
    coefs = exchange(jnp.broadcast_to(coef[None], (rows,) + coef.shape), "row")

    parity = (lax.axis_index("col") % 2).astype(jnp.int32).reshape(1)
    own, other = interpolate(parity, counts, lists, node_data, centre_data, coefs)
    other = lax.ppermute(other, "col", [(c, c ^ 1) for c in range(cols)])
    both = (own.astype(jnp.float32) + other.astype(jnp.float32)).astype(jnp.bfloat16)
    chips = [[c for c in range(cols) if c % 2 == core] for core in range(2)]
    both = lax.all_to_all(
        both, "col", split_axis=0, concat_axis=0, axis_index_groups=chips, tiled=True
    )
    return restore(both, node_rank[None, :], disp_rows)


def solution(mesh):
    placed = (
        P(None, ("row", "col")),
        P(("row", "col")),
        P("row", "col"),
        P(),
        P(None, ("row", "col")),
    )
    return jax.shard_map(per_device, mesh=mesh, in_specs=placed, out_specs=P(None, ("row", "col")), check_vma=False)
```
